32 devices in a mesh: wide: 16 (over z, y, core), narrow: 2 (over x).
Axes of the slice: x: 2, y: 2, z: 4, core: 2. Of those that a mesh axis runs over, the one named last changes fastest.
Arguments:
- patches: bfloat16 [32768, 768], P(('wide', 'narrow')), may hold values from -6 to 6
- conditions: bfloat16 [128, 768], P(('wide', 'narrow')), as said below
- modulation_weight: bfloat16 [768, 4608], P('narrow', 'wide'), may hold values from -0.21875 to 0.21875
- attention_weight: bfloat16 [768, 2304], P('narrow', 'wide'), may hold values from -0.21875 to 0.21875
- projection_weight: bfloat16 [768, 768], P('narrow', 'wide'), may hold values from -3.5 to 3.5
- expand_weight: bfloat16 [768, 3072], P('narrow', 'wide'), may hold values from -0.21875 to 0.21875
- contract_weight: bfloat16 [3072, 768], P('narrow', 'wide'), may hold values from -0.109375 to 0.109375
- expert_expand: bfloat16 [16, 768, 3072], P('wide', 'narrow'), may hold values from -0.21875 to 0.21875
- expert_contract: bfloat16 [16, 3072, 768], P('wide', 'narrow'), may hold values from -0.21875 to 0.21875
- image_start: int32 [32768], P('wide'), may hold values from 0 to 127, as said below
- routes: int32 [32768, 2], P(('wide', 'narrow')), may hold values from 0 to 15, all different within a row; in each aligned block of 1024 rows (0 to 1023, 1024 to 2047, ...) at most 256 rows name the same one
- route_gates: float32 [32768, 2], P(('wide', 'narrow')), may hold values from 0.1 to 0.9
- cotangent: bfloat16 [32768, 768], P(('wide', 'narrow')), may hold values from -6 to 6
Outputs:
- block_out: bfloat16 [32768, 768], P(('wide', 'narrow'))
- patch_grad: bfloat16 [32768, 768], P(('wide', 'narrow'))
- modulation_grad: float32 [768, 4608], P('narrow', 'wide')
- attention_grad: float32 [768, 2304], P('narrow', 'wide')
- projection_grad: float32 [768, 768], P('narrow', 'wide')
- expand_grad: float32 [768, 3072], P('narrow', 'wide')
- contract_grad: float32 [3072, 768], P('narrow', 'wide')
- expert_expand_grad: float32 [16, 768, 3072], P('wide', 'narrow')
- expert_contract_grad: float32 [16, 3072, 768], P('wide', 'narrow')
The draws below stay inside these ranges and needn't reach their ends.
Inputs may be any that keep to these rules, and one draw needn't show every extreme that they name: `image_start`: each aligned group of 2048 patches begins with one image that starts at the group's first patch and ends within the group's last 1024 patches, a whole number of blocks of 256; the group's remaining patches are images of 256 patches; every patch of an image holds the index of the image's first block of 256 patches. `conditions`: all blocks of one image have equal rows. `routes`: each row names two different experts; among the rows of one device at most 256 choices name one expert, and exactly 256 do for some expert in every draw; every expert is named.
All inputs are finite; a program needn't handle non-finite values.
Results may differ from the reference program's by a relative error of at most 0.015.
Values may be sent and summed in bfloat16 or wider, within the bound.
No kernel may reach another device: no remote copies, remote signals or barrier semaphores. Data moves between devices by JAX's collectives and lax.ppermute only.
A program may use at most 384 MiB of HBM per device.

```python
import math
import jax
import jax.numpy as jnp
import numpy as np
from jax import lax

D = 768
HEADS = 12
FF = 3072
GROUP_TOK = 2048
IMG_SHORT = 256
TOK_DEV = 1024
TOKENS = 32768
SLOTS = 128
EXPERTS = 16
CAP = 256
N_WIDE = 16
N_NARROW = 2


def image_layout(key):
    groups = TOKENS // GROUP_TOK
    per_group = GROUP_TOK // IMG_SHORT
    per_device = TOK_DEV // IMG_SHORT
    shorts = jax.random.randint(jax.random.fold_in(key, 101), (groups,), 0, per_device)
    slot_index = jnp.arange(SLOTS, dtype=jnp.int32)
    group = slot_index // per_group
    within = slot_index % per_group
    long_blocks = per_group - shorts[group]
    first = jnp.where(within < long_blocks, group * per_group, slot_index)
    return first.astype(jnp.int32)


def draw_image_start(key, part):
    first = image_layout(key)
    return jnp.repeat(first, IMG_SHORT).astype(jnp.int32)


def draw_conditions(key, part):
    first = image_layout(key)
    inner_key = jax.random.fold_in(key, 202)
    base = jax.random.normal(inner_key, (SLOTS, D), jnp.float32)
    return base[first].astype(jnp.bfloat16)


def shard_levels(stream_key, shape, shards, smallest, largest):
    gain, own = 1.0, jax.random.fold_in(stream_key, 6)
    for axis_at, blocks in shards:
        heights = jnp.exp(jax.random.uniform(jax.random.fold_in(own, axis_at), (blocks,), jnp.float32, smallest / len(shards), largest / len(shards)))
        gain = gain * jnp.repeat(heights, shape[axis_at] // blocks).reshape([-1 if axis == axis_at else 1 for axis in range(len(shape))])
    return gain


def routed_block(rng, own, number, rows, count, top, bound, skew):
    order = jax.random.permutation(rng, count)
    packed, usual = shares(count, rows * top, bound, skew, True), shares(count, rows * top, bound, skew, False)
    places = jnp.arange(count)

    def named(tallies, offset_by):
        used = int((tallies > 0).sum())
        fixed = max(1, used // 4)
        shifted = fixed + (places - fixed + offset_by * (used - fixed)) % max(1, count - fixed)
        return jnp.zeros((count,), jnp.int32).at[order[jnp.where(places < fixed, places, shifted)]].set(jnp.asarray(tallies, jnp.int32))

    tallies = jnp.where(number % 4 == 0, named(packed, number // 4), named(usual, number - number // 4 - 1))
    mixed = jax.random.permutation(jax.random.fold_in(own, 3), count)
    source_of, taker = mixed[0:count // 2 * 2:2], mixed[1:count // 2 * 2:2]
    slack = jnp.minimum(tallies[source_of] - 1, bound - tallies[taker]) // 2
    slack = jnp.where((source_of == order[0]) | (taker == order[0]) | (tallies[taker] == 0), 0, jnp.maximum(slack, 0))
    shifted = jax.random.randint(jax.random.fold_in(own, 4), (count // 2,), 0, 1 << 20) % (slack + 1)
    tallies = tallies.at[source_of].add(-shifted).at[taker].add(shifted)
    labels = jnp.searchsorted(jnp.cumsum(tallies), jnp.arange(rows * top), side="right").astype(jnp.int32)
    grid = labels.reshape(top, rows).T
    grid = grid[jax.random.permutation(jax.random.fold_in(own, 1), rows)]
    offset_by = jax.random.randint(jax.random.fold_in(own, 2), (rows, 1), 0, top)
    return jnp.take_along_axis(grid, (jnp.arange(top)[None, :] + offset_by) % top, axis=1)


def shares(number_of, total, bound, lean, full):
    portions = [(1 << 20) // math.isqrt(rank ** lean) + 1 for rank in range(1, number_of + 1)]
    largest = bound if full else min(bound, max(-(-total // number_of), total * portions[0] // sum(portions)))
    least = 1 if total - largest >= number_of - 1 else 0
    counts, surplus = [largest] + [least] * (number_of - 1), total - largest - least * (number_of - 1)
    while surplus > 0:
        free = [i for i in range(1, number_of) if counts[i] < largest] or [i for i in range(1, number_of) if counts[i] < bound]
        whole, left = sum([portions[i] for i in free]), surplus
        for i in free:
            more = min(bound - counts[i], max(1, left * portions[i] // whole), surplus)
            counts[i] = counts[i] + more
            surplus = surplus - more
    return np.array(counts)


def noise(key, shape, deviation, most, shards=(), kind=jnp.bfloat16):
    values = jax.random.normal(key, shape, jnp.float32) * deviation
    if len(shards) > 0:
        values = shard_levels(key, shape, shards, -0.22, 0.18) * values
    return jnp.clip(values, min=-most, max=most).astype(kind)


def setup_inputs(seed: int = 0) -> dict:
    streams_of = jax.random.split(jax.random.key(seed), 14)
    patches = noise(streams_of[0], (TOKENS, D), 1.0, 6.0, ((0, 32),))
    conditions = draw_conditions(jax.random.fold_in(streams_of[13], 71), 0)
    modulation_weight = noise(streams_of[2], (D, 6 * D), D ** -0.5, 0.21875, ((0, 2), (1, 16)))
    attention_weight = noise(streams_of[3], (D, 3 * D), D ** -0.5, 0.21875, ((0, 2), (1, 16)))
    projection_weight = noise(streams_of[4], (D, D), (max(1, D // 256)) ** -0.5, 3.5, ((0, 2), (1, 16)))
    expand_weight = noise(streams_of[5], (D, FF), D ** -0.5, 0.21875, ((0, 2), (1, 16)))
    contract_weight = noise(streams_of[6], (FF, D), FF ** -0.5, 0.109375, ((0, 2), (1, 16)))
    expert_expand = noise(streams_of[7], (EXPERTS, D, FF), D ** -0.5, 0.21875, ((0, 16), (1, 2)))
    expert_contract = noise(streams_of[8], (EXPERTS, FF, D), (FF // 4) ** -0.5, 0.21875, ((0, 16), (1, 2)))
    image_start = draw_image_start(jax.random.fold_in(streams_of[13], 71), 0)
    routes_keys = jax.random.split(jax.random.fold_in(streams_of[10], 1), TOKENS // TOK_DEV)
    routes_turns = jax.random.permutation(jax.random.fold_in(streams_of[10], 3), TOKENS // TOK_DEV)
    routes = jax.vmap(lambda own, number: routed_block(jax.random.fold_in(streams_of[10], 2), own, number, TOK_DEV, EXPERTS, 2, CAP, 2))(routes_keys, routes_turns).reshape((TOKENS, 2))
    route_gates = jnp.clip(0.1 + 0.79999997 * jax.random.uniform(streams_of[11], (TOKENS, 2), jnp.float32) ** shard_levels(streams_of[11], (TOKENS, 2), ((0, 32),), -0.2, 0.2), 0.1, 0.9)
    cotangent = noise(streams_of[12], (TOKENS, D), 1.0, 6.0, ((0, 32),))
    return {"patches": patches, "conditions": conditions, "modulation_weight": modulation_weight, "attention_weight": attention_weight, "projection_weight": projection_weight, "expand_weight": expand_weight, "contract_weight": contract_weight, "expert_expand": expert_expand, "expert_contract": expert_contract, "image_start": image_start, "routes": routes, "route_gates": route_gates, "cotangent": cotangent}


@jax.custom_vjp
def low(v):
    return lax.optimization_barrier(v.astype(jnp.bfloat16)).astype(jnp.float32)

@jax.custom_vjp
def low_back(v):
    return v

def low_keep(v):
    return (low(v), None)

def low_pass(kept, grad):
    return (grad,)

def back_keep(v):
    return (v, None)

def back_low(kept, grad):
    return (low(grad),)
low.defvjp(low_keep, low_pass)
low_back.defvjp(back_keep, back_low)
EPSILON = 1e-06
HIGHEST = lax.Precision.HIGHEST

def matmul(left, right):
    return jnp.dot(left, right, precision=HIGHEST, preferred_element_type=jnp.float32)

def normalize(values):
    centered = values - lax.optimization_barrier(jnp.mean(values, axis=-1, keepdims=True))
    variance = lax.optimization_barrier(jnp.mean(centered * centered, axis=-1, keepdims=True))
    return centered * lax.rsqrt(variance + EPSILON)

def image_attention(queries, keys_in, values_in, starts):
    score_scale = (D // HEADS) ** (-0.5)
    scores = low_back(jnp.einsum('qhd,khd->hqk', queries, keys_in, precision=HIGHEST) * score_scale)
    same_image = (starts[:, None] == starts[None, :])[None]
    scores = jnp.where(same_image, scores, -1e+30)
    weights = low(jax.nn.softmax(scores, axis=-1))
    return jnp.einsum('hqk,khd->qhd', weights, values_in, precision=HIGHEST)

def front_half(patch_group, span_group, start_group, attention_w, projection_w, expand_w, contract_w):
    shift_a = span_group[:, 0]
    scale_a = span_group[:, 1]
    gate_a = span_group[:, 2]
    shift_b = span_group[:, 3]
    scale_b = span_group[:, 4]
    head_dim = D // HEADS
    first_entry = low(normalize(patch_group) * (1.0 + scale_a) + shift_a).reshape(GROUP_TOK, D)
    triple = low(low_back(matmul(first_entry, attention_w)))
    queries = triple[:, :D].reshape(GROUP_TOK, HEADS, head_dim)
    keys_in = triple[:, D:2 * D].reshape(GROUP_TOK, HEADS, head_dim)
    values_in = triple[:, 2 * D:].reshape(GROUP_TOK, HEADS, head_dim)
    mixed_heads = image_attention(queries, keys_in, values_in, start_group).reshape(GROUP_TOK, D)
    mixed_heads = low(low_back(mixed_heads))
    attended = low_back(matmul(mixed_heads, projection_w)).reshape(patch_group.shape)
    middle = patch_group + gate_a * attended
    second = low(normalize(middle) * (1.0 + scale_b) + shift_b).reshape(GROUP_TOK, D)
    hidden = low_back(matmul(second, expand_w))
    shared = low_back(matmul(low(jax.nn.gelu(hidden)), contract_w))
    return (middle, second, shared)

def reference(patches, conditions, modulation_weight, attention_weight, projection_weight, expand_weight, contract_weight, expert_expand, expert_contract, image_start, routes, route_gates, cotangent):
    flat_routes = routes.reshape(-1).astype(jnp.int32)
    limit = CAP * N_WIDE * N_NARROW

    def expert_rows(expert):
        return jnp.nonzero(flat_routes == expert, size=limit, fill_value=2 * TOKENS)[0].astype(jnp.int32)
    table = lax.map(expert_rows, jnp.arange(EXPERTS, dtype=jnp.int32))
    gate_values = route_gates.astype(jnp.float32)
    group_count = TOKENS // GROUP_TOK
    per_group = GROUP_TOK // IMG_SHORT

    def forward(patch_values, cond_values, modulation_w, attention_w, projection_w, expand_w, contract_w, up_all, down_all):
        lifted = low(jax.nn.silu(cond_values))
        modulation = low_back(matmul(lifted, modulation_w)).reshape(SLOTS, 6, 1, D)
        patch_groups = patch_values.reshape(group_count, per_group, IMG_SHORT, D)
        span_groups = modulation.reshape(group_count, per_group, 6, 1, D)
        start_groups = image_start.reshape(group_count, GROUP_TOK)

        def run_group(items):
            return front_half(items[0], items[1], items[2], attention_w, projection_w, expand_w, contract_w)
        middle, second, shared = lax.map(jax.checkpoint(run_group), (patch_groups, span_groups, start_groups))
        pairs = jnp.repeat(second.reshape(TOKENS, D), 2, axis=0)
        padded = jnp.concatenate([pairs, jnp.zeros((1, D), pairs.dtype)], axis=0)

        def run_expert(items):
            picks, up_w, down_w = items
            rows_in = low_back(padded[picks])
            expert_hidden = low_back(matmul(rows_in, up_w))
            return low(low_back(matmul(low(jax.nn.gelu(expert_hidden)), down_w)))
        expert_out = lax.map(jax.checkpoint(run_expert), (table, up_all, down_all))
        combined = jnp.zeros((2 * TOKENS + 1, D), expert_out.dtype).at[table.reshape(-1)].add(expert_out.reshape(-1, D))
        routed = combined[:2 * TOKENS].reshape(TOKENS, 2, D)
        mixture = shared.reshape(TOKENS, D) + lax.optimization_barrier(jnp.sum(gate_values[:, :, None] * routed, axis=1))
        gate_b = modulation[:, 5]
        result = middle.reshape(SLOTS, IMG_SHORT, D) + gate_b * mixture.reshape(SLOTS, IMG_SHORT, D)
        return result.reshape(TOKENS, D)
    floats = tuple((member.astype(jnp.float32) for member in (patches, conditions, modulation_weight, attention_weight, projection_weight, expand_weight, contract_weight, expert_expand, expert_contract)))
    result, pullback = jax.vjp(forward, *floats)
    grads = pullback(cotangent.astype(jnp.float32))
    return (result.astype(jnp.bfloat16), grads[0].astype(jnp.bfloat16), grads[2], grads[3], grads[4], grads[5], grads[6], grads[7], grads[8])
```

```python
import functools

import jax
import jax.numpy as jnp
from jax import lax
from jax.experimental import pallas as pl
from jax.experimental.pallas import tpu as pltpu
from jax.sharding import PartitionSpec as P

HEADS = 12
IMG_SHORT = 256
EPSILON = 1e-06
QUAD = 4
F32 = jnp.float32
BF16 = jnp.bfloat16
NN = (((1,), (0,)), ((), ()))
NT = (((1,), (1,)), ((), ()))
VMEM_BYTES = 48 << 20


def dot(left, right, dims=NN):
    return lax.dot_general(left, right, dims, preferred_element_type=F32)


def product(left, right, form):
    return jnp.einsum(form, left, right, preferred_element_type=F32)


def normalize(values):
    centered = values - jnp.mean(values, axis=-1, keepdims=True)
    variance = jnp.mean(centered * centered, axis=-1, keepdims=True)
    return centered * lax.rsqrt(variance + EPSILON)


def norm_back(values, grad_normed):
    centered = values - jnp.mean(values, axis=-1, keepdims=True)
    variance = jnp.mean(centered * centered, axis=-1, keepdims=True)
    inverse = lax.rsqrt(variance + EPSILON)
    normed = centered * inverse
    return inverse * (
        grad_normed
        - jnp.mean(grad_normed, axis=-1, keepdims=True)
        - normed * jnp.mean(grad_normed * normed, axis=-1, keepdims=True)
    )


def of_head(values, which, axis, head_dim):
    place = lax.broadcasted_iota(jnp.int32, values.shape, axis) // head_dim
    return jnp.where(place == which, values, jnp.zeros_like(values))


def over_blocks(low, high, all_blocks, step, state):
    def unrolled():
        inner = state
        for block in range(all_blocks):
            inner = step(block, inner)
        return inner

    def several(count):
        def body(index, inner):
            for extra in range(count):
                inner = step(low + index * count + extra, inner)
            return inner

        return body

    def looped():
        groups = (high - low) // 4
        inner = lax.fori_loop(0, groups, several(4), state)
        return lax.fori_loop(low + groups * 4, high, step, inner)

    return lax.cond(high - low == all_blocks, unrolled, looped)


def at_block(block, size):
    return block * size if isinstance(block, int) else pl.multiple_of(block * size, size)


def forward_kernel(
    head_dim, size, low_ref, high_ref, q_ref, k_ref, v_ref, out_ref, exact_ref, total_ref, vt, kept
):
    row_block = pl.program_id(1)

    @pl.when(row_block == 0)
    def _():
        vt[...] = v_ref[...].T

    queries = (q_ref[...].astype(F32) * head_dim**-0.5).astype(BF16).T
    rows = q_ref.shape[0]
    by_head = [of_head(queries, h, 0, head_dim) for h in range(QUAD)]
    low, high = low_ref[row_block], high_ref[row_block]
    blocks = k_ref.shape[0] // size

    def score_step(block, tops):
        at = at_block(block, size)
        keys = k_ref[pl.ds(at, size), :]
        fresh = []
        for h in range(QUAD):
            scores = dot(keys, by_head[h])
            kept[h, pl.ds(at, size), :] = scores
            fresh.append(
                jnp.maximum(tops[h], jnp.max(scores.reshape(size // 8, 8, rows), axis=0))
            )
        return tuple(fresh)

    tops = over_blocks(
        low, high, blocks, score_step, tuple(jnp.full((8, rows), -1e30, F32) for _ in range(QUAD))
    )
    tops = [jnp.max(t, axis=0, keepdims=True) for t in tops]

    def mix_step(block, state):
        at = at_block(block, size)
        fresh = []
        for h in range(QUAD):
            total, mixed = state[h]
            weights = jnp.exp(kept[h, pl.ds(at, size), :] - tops[h])
            total = total + jnp.sum(weights.reshape(size // 8, 8, rows), axis=0)
            values = vt[h * head_dim : (h + 1) * head_dim, pl.ds(at, size)]
            fresh.append((total, mixed + dot(values, weights.astype(BF16))))
        return tuple(fresh)

    state = over_blocks(
        low,
        high,
        blocks,
        mix_step,
        tuple((jnp.zeros((8, rows), F32), jnp.zeros((head_dim, rows), F32)) for _ in range(QUAD)),
    )
    mixed = []
    for h in range(QUAD):
        total = jnp.sum(state[h][0], axis=0, keepdims=True)
        mixed.append(state[h][1] / total)
        total_ref[0, h : h + 1, :] = tops[h] + jnp.log(total)
    mixed = jnp.concatenate(mixed, axis=0).T
    exact_ref[...] = mixed
    out_ref[...] = mixed.astype(BF16)


def attention_forward(queries, keys, values, low, high):
    rows, width = queries.shape
    key_rows = keys.shape[0]
    head_dim = width // HEADS
    lanes, quads = QUAD * head_dim, HEADS // QUAD
    size = IMG_SHORT
    row_spec = pl.BlockSpec((size, lanes), lambda j, i, *_: (i, j))
    key_spec = pl.BlockSpec((key_rows, lanes), lambda j, i, *_: (0, j))
    return pl.pallas_call(
        functools.partial(forward_kernel, head_dim, size),
        grid_spec=pltpu.PrefetchScalarGridSpec(
            num_scalar_prefetch=2,
            grid=(quads, rows // size),
            in_specs=[row_spec, key_spec, key_spec],
            out_specs=[
                row_spec,
                row_spec,
                pl.BlockSpec((1, QUAD, size), lambda j, i, *_: (j, 0, i)),
            ],
            scratch_shapes=[
                pltpu.VMEM((lanes, key_rows), BF16),
                pltpu.VMEM((QUAD, key_rows, size), F32),
            ],
        ),
        out_shape=[
            jax.ShapeDtypeStruct((rows, width), BF16),
            jax.ShapeDtypeStruct((rows, width), F32),
            jax.ShapeDtypeStruct((quads, QUAD, rows), F32),
        ],
        compiler_params=pltpu.CompilerParams(vmem_limit_bytes=VMEM_BYTES),
        cost_estimate=pl.CostEstimate(
            flops=16 * rows * key_rows * width,
            transcendentals=rows * key_rows * HEADS,
            bytes_accessed=4 * key_rows * width + 8 * rows * width,
        ),
        name="attention_forward",
    )(low, high, queries, keys, values)


def backward_kernel(
    head_dim,
    size,
    low_ref,
    high_ref,
    q_ref,
    k_ref,
    v_ref,
    grad_ref,
    exact_ref,
    total_ref,
    dq_ref,
    dk_ref,
    dv_ref,
    kt,
    dk_sum,
    dv_sum,
):
    row_block = pl.program_id(1)

    @pl.when(row_block == 0)
    def _():
        kt[...] = k_ref[...].T
        dk_sum[...] = jnp.zeros_like(dk_sum)
        dv_sum[...] = jnp.zeros_like(dv_sum)

    scale = head_dim**-0.5
    queries = (q_ref[...].astype(F32) * scale).astype(BF16)
    grads = grad_ref[...]
    rows = queries.shape[0]
    heads = range(QUAD)
    dots = (grads.astype(F32) * exact_ref[...]).T
    dots = [
        jnp.sum(dots[h * head_dim : (h + 1) * head_dim], axis=0, keepdims=True) for h in heads
    ]
    q_columns, g_columns = queries.T, grads.T
    q_columns = [of_head(q_columns, h, 0, head_dim) for h in heads]
    g_columns = [of_head(g_columns, h, 0, head_dim) for h in heads]
    q_rows = jnp.concatenate([of_head(queries, h, 1, head_dim) for h in heads], axis=0)
    g_rows = jnp.concatenate([of_head(grads, h, 1, head_dim) for h in heads], axis=0)
    totals = [total_ref[0, h : h + 1, :] for h in heads]
    low, high = low_ref[row_block], high_ref[row_block]
    blocks = k_ref.shape[0] // size

    def step(block, dq):
        at = at_block(block, size)
        keys = k_ref[pl.ds(at, size), :]
        values = v_ref[pl.ds(at, size), :]
        weights, score_grads, fresh = [], [], []
        for h in heads:
            softmax = jnp.exp(dot(keys, q_columns[h]) - totals[h])
            grad = (softmax * (dot(values, g_columns[h]) - dots[h])).astype(BF16)
            weights.append(softmax.astype(BF16))
            score_grads.append(grad)
            columns = kt[h * head_dim : (h + 1) * head_dim, pl.ds(at, size)]
            fresh.append(dq[h] + dot(columns, grad))
        dv_sum[pl.ds(at, size), :] += dot(jnp.concatenate(weights, axis=1), g_rows)
        dk_sum[pl.ds(at, size), :] += dot(jnp.concatenate(score_grads, axis=1), q_rows)
        return tuple(fresh)

    dq = over_blocks(
        low, high, blocks, step, tuple(jnp.zeros((head_dim, rows), F32) for _ in heads)
    )
    dq_ref[...] = (jnp.concatenate(dq, axis=0) * scale).T.astype(BF16)

    @pl.when(row_block == pl.num_programs(1) - 1)
    def _():
        dk_ref[...] = dk_sum[...].astype(BF16)
        dv_ref[...] = dv_sum[...].astype(BF16)


def attention_backward(queries, keys, values, grads, exact, totals, low, high):
    rows, width = queries.shape
    key_rows = keys.shape[0]
    head_dim = width // HEADS
    lanes, quads = QUAD * head_dim, HEADS // QUAD
    size = IMG_SHORT
    row_spec = pl.BlockSpec((size, lanes), lambda j, i, *_: (i, j))
    key_spec = pl.BlockSpec((key_rows, lanes), lambda j, i, *_: (0, j))
    return pl.pallas_call(
        functools.partial(backward_kernel, head_dim, size),
        grid_spec=pltpu.PrefetchScalarGridSpec(
            num_scalar_prefetch=2,
            grid=(quads, rows // size),
            in_specs=[
                row_spec,
                key_spec,
                key_spec,
                row_spec,
                row_spec,
                pl.BlockSpec((1, QUAD, size), lambda j, i, *_: (j, 0, i)),
            ],
            out_specs=[row_spec, key_spec, key_spec],
            scratch_shapes=[
                pltpu.VMEM((lanes, key_rows), BF16),
                pltpu.VMEM((key_rows, lanes), F32),
                pltpu.VMEM((key_rows, lanes), F32),
            ],
        ),
        out_shape=[
            jax.ShapeDtypeStruct((rows, width), BF16),
            jax.ShapeDtypeStruct((key_rows, width), BF16),
            jax.ShapeDtypeStruct((key_rows, width), BF16),
        ],
        compiler_params=pltpu.CompilerParams(vmem_limit_bytes=VMEM_BYTES),
        cost_estimate=pl.CostEstimate(
            flops=40 * rows * key_rows * width,
            transcendentals=rows * key_rows * HEADS,
            bytes_accessed=8 * key_rows * width + 10 * rows * width,
        ),
        name="attention_backward",
    )(low, high, queries, keys, values, grads, exact, totals)


def pack_kernel(place_ref, scale_ref, values_ref, out_ref):
    expert = pl.program_id(0)
    capacity = out_ref.shape[0]
    places = place_ref[pl.ds(expert, 1), :]
    slots = lax.broadcasted_iota(jnp.int32, (capacity, places.shape[1]), 0)
    chosen = slots == places
    rows = dot(chosen.astype(BF16), values_ref[...])
    if scale_ref is not None:
        scales = jnp.where(chosen, scale_ref[pl.ds(expert, 1), :], 0.0)
        rows = rows * jnp.sum(scales, axis=1, keepdims=True)
    out_ref[...] = rows.astype(BF16)


def pack(places, scales, values, capacity):
    experts, rows = places.shape
    width = values.shape[1]
    whole = lambda shape: pl.BlockSpec(shape, lambda e: (0, 0))
    operands = [places, values] if scales is None else [places, scales, values]
    kernel = pack_kernel
    if scales is None:
        kernel = lambda place_ref, values_ref, out_ref: pack_kernel(
            place_ref, None, values_ref, out_ref
        )
    return pl.pallas_call(
        kernel,
        grid=(experts,),
        in_specs=[whole(o.shape) for o in operands],
        out_specs=pl.BlockSpec((capacity, width), lambda e: (e, 0)),
        out_shape=jax.ShapeDtypeStruct((experts * capacity, width), BF16),
        compiler_params=pltpu.CompilerParams(vmem_limit_bytes=VMEM_BYTES),
        cost_estimate=pl.CostEstimate(
            flops=2 * experts * capacity * rows * width,
            transcendentals=0,
            bytes_accessed=2 * width * (rows + experts * capacity),
        ),
        name="pack",
    )(*operands)


def combine_kernel(experts, capacity, place_ref, scale_ref, rows_ref, out_ref):
    total = None
    tokens = out_ref.shape[0]
    slots = lax.broadcasted_iota(jnp.int32, (tokens, capacity), 1)
    for expert in range(experts):
        scale = 1.0 if scale_ref is None else scale_ref[:, expert : expert + 1]
        chosen = jnp.where(slots == place_ref[:, expert : expert + 1], scale, 0.0)
        part = dot(chosen.astype(BF16), rows_ref[expert * capacity : (expert + 1) * capacity, :])
        total = part if total is None else total + part
    out_ref[...] = total


def combine(places, scales, rows, capacity):
    tokens, experts = places.shape
    width = rows.shape[1]
    block = min(256, tokens)
    part = pl.BlockSpec((block, experts), lambda i: (i, 0))
    kernel = functools.partial(combine_kernel, experts, capacity)
    operands = [places, rows] if scales is None else [places, scales, rows]
    if scales is None:
        kernel = lambda place_ref, rows_ref, out_ref: combine_kernel(
            experts, capacity, place_ref, None, rows_ref, out_ref
        )
    return pl.pallas_call(
        kernel,
        grid=(tokens // block,),
        in_specs=[part] * (len(operands) - 1)
        + [pl.BlockSpec(rows.shape, lambda i: (0, 0), pipeline_mode=pl.Buffered(1))],
        out_specs=pl.BlockSpec((block, width), lambda i: (i, 0)),
        out_shape=jax.ShapeDtypeStruct((tokens, width), F32),
        compiler_params=pltpu.CompilerParams(vmem_limit_bytes=VMEM_BYTES),
        cost_estimate=pl.CostEstimate(
            flops=2 * experts * capacity * tokens * width,
            transcendentals=0,
            bytes_accessed=2 * width * (2 * tokens + experts * capacity),
        ),
        name="combine",
    )(*operands)


def gelu_both(hidden):
    inner = 0.7978845608028654
    square = hidden * hidden
    bend = jnp.tanh(hidden * (inner + (inner * 0.044715) * square))
    half = 0.5 + 0.5 * bend
    slope = half + (0.5 * hidden) * (1.0 - bend * bend) * (inner + (3 * inner * 0.044715) * square)
    return hidden * half, slope


def feed_kernel(
    transposed, tile, with_out, in_ref, grad_ref, up_ref, down_ref, act_ref, hid_ref, back_ref, *out
):
    rows, grads = in_ref[...], grad_ref[...]
    hidden_size = act_ref.shape[1]
    for start in range(0, hidden_size, tile):
        part = slice(start, start + tile)
        if transposed:
            hidden = dot(rows, up_ref[part, :], NT)
            grad = dot(grads, down_ref[:, part])
        else:
            hidden = dot(rows, up_ref[:, part])
            grad = dot(grads, down_ref[part, :], NT)
        active, slope = gelu_both(hidden)
        act_ref[:, part] = active.astype(BF16)
        hid_ref[:, part] = (grad * slope).astype(BF16)
    back = dot(hid_ref[...], up_ref[...], NN if transposed else NT)
    back_ref[...] = back.astype(back_ref.dtype)
    if with_out:
        out[0][...] = dot(act_ref[...], down_ref[...], NT if transposed else NN).astype(
            out[0].dtype
        )


def feed(rows, grads, up, down, transposed, out_dtype, with_out):
    count, width = rows.shape
    hidden_size = up.shape[0] if transposed else up.shape[1]
    block = min(256, count)
    row = pl.BlockSpec((block, width), lambda i: (i, 0))
    hid = pl.BlockSpec((block, hidden_size), lambda i: (i, 0))
    fixed = lambda a: pl.BlockSpec(a.shape, lambda i: (0, 0), pipeline_mode=pl.Buffered(1))
    extra = 1 if with_out else 0
    return pl.pallas_call(
        functools.partial(feed_kernel, transposed, min(512, hidden_size), with_out),
        grid=(count // block,),
        in_specs=[row, row, fixed(up), fixed(down)],
        out_specs=[hid, hid, row] + [row] * extra,
        out_shape=[
            jax.ShapeDtypeStruct((count, hidden_size), BF16),
            jax.ShapeDtypeStruct((count, hidden_size), BF16),
            jax.ShapeDtypeStruct((count, width), out_dtype),
        ]
        + [jax.ShapeDtypeStruct((count, width), out_dtype)] * extra,
        compiler_params=pltpu.CompilerParams(vmem_limit_bytes=VMEM_BYTES),
        cost_estimate=pl.CostEstimate(
            flops=(6 + 2 * extra) * count * width * hidden_size,
            transcendentals=count * hidden_size,
            bytes_accessed=4 * count * hidden_size + 8 * count * width + 4 * width * hidden_size,
        ),
        name="feed",
    )(rows, grads, up, down)


def swap(values):
    return lax.ppermute(values, "narrow", [(0, 1), (1, 0)])


def gather_narrow(values, axis):
    if lax.axis_size("narrow") != 2:
        return lax.all_gather(values, "narrow", axis=axis, tiled=True)
    other = swap(values)
    return jnp.where(
        lax.axis_index("narrow") == 0,
        jnp.concatenate([values, other], axis=axis),
        jnp.concatenate([other, values], axis=axis),
    )


def part_of(values, index, size, axis):
    return lax.dynamic_slice_in_dim(values, index * size, size, axis)


def reduce_narrow(values, axis):
    count = lax.axis_size("narrow")
    if count != 2:
        return lax.psum_scatter(
            values.astype(BF16), "narrow", scatter_dimension=axis, tiled=True
        ).astype(F32)
    size = values.shape[axis] // 2
    index = lax.axis_index("narrow")
    other = swap(part_of(values, 1 - index, size, axis).astype(BF16))
    return part_of(values, index, size, axis).astype(F32) + other.astype(F32)


def exchange(rows):
    wide = lax.axis_size("wide")
    blocks = rows.reshape(wide, rows.shape[0] // wide, rows.shape[1])
    return lax.all_to_all(blocks, "wide", split_axis=0, concat_axis=0, tiled=True).reshape(
        rows.shape
    )


def gather_wide(values):
    return lax.all_gather(values, "wide", axis=0, tiled=True)


def reduce_wide(values):
    return lax.psum_scatter(values, "wide", scatter_dimension=0, tiled=True)


def on_device(
    patches,
    conditions,
    modulation_weight,
    attention_weight,
    projection_weight,
    expand_weight,
    contract_weight,
    expert_expand,
    expert_contract,
    image_start,
    routes,
    route_gates,
    cotangent,
):
    local_rows, width = patches.shape
    slots = conditions.shape[0]
    experts = lax.axis_size("wide")
    narrow = lax.axis_size("narrow")
    capacity = 4 * local_rows // experts
    mine = lax.axis_index("narrow")
    group_slots = narrow * slots
    group_rows = narrow * local_rows

    attention_t = gather_wide(gather_narrow(attention_weight.T, 1))
    modulation_columns = gather_narrow(modulation_weight, 0)
    group_patches = gather_narrow(patches, 0)
    projection_t = gather_wide(gather_narrow(projection_weight.T, 1))
    expand_t = gather_wide(gather_narrow(expand_weight.T, 1))
    contract_t = gather_wide(gather_narrow(contract_weight.T, 1))
    up = gather_narrow(expert_expand[0], 0)
    down = gather_narrow(expert_contract[0], 0)

    all_conditions = lax.all_gather(conditions, ("wide", "narrow"), axis=0, tiled=True)
    lifted = jax.nn.silu(all_conditions.astype(F32)).astype(BF16)
    columns = jnp.dot(lifted, modulation_columns, preferred_element_type=F32)
    share = columns.shape[1]
    modulation = lax.all_to_all(
        columns.reshape(experts, group_slots, share), "wide", split_axis=0, concat_axis=0, tiled=True
    )
    modulation = modulation.transpose(1, 0, 2).reshape(group_slots, 6, 1, width)
    own = part_of(modulation, mine, slots, 0)
    shift_a, scale_a, gate_a, shift_b, scale_b, gate_b = [own[:, i] for i in range(6)]

    expert_ids = jnp.arange(experts, dtype=jnp.int32)[None, :]
    named = routes[:, :, None] == expert_ids[None]
    chosen = jnp.any(named, axis=1)
    order = jnp.arange(local_rows, dtype=jnp.int32)
    earlier = (order[:, None] > order[None, :]).astype(BF16)
    rank = jnp.dot(earlier, chosen.astype(BF16), preferred_element_type=F32).astype(jnp.int32)
    places = jnp.where(chosen, rank, -1)
    gates = jnp.sum(jnp.where(named, route_gates[:, :, None], 0.0), axis=1)
    places_t, gates_t = places.T, gates.T

    grad_top = cotangent.astype(F32).reshape(slots, IMG_SHORT, width)
    grad_shared = (gate_b * grad_top).astype(BF16).reshape(local_rows, width)
    grad_arrived = exchange(pack(places_t, gates_t, grad_shared, capacity))

    block_start = image_start.reshape(group_slots, IMG_SHORT)[:, 0]
    own_start = part_of(block_start, mine, slots, 0)
    low = own_start - block_start[0]
    high = low + jnp.sum(own_start[:, None] == block_start[None, :], axis=1, dtype=jnp.int32)
    group_inputs = group_patches.astype(F32).reshape(group_slots, IMG_SHORT, width)
    group_entry = (
        (normalize(group_inputs) * (1.0 + modulation[:, 1]) + modulation[:, 0])
        .astype(BF16)
        .reshape(group_rows, width)
    )
    first_entry = part_of(group_entry, mine, local_rows, 0)
    query_t, key_value_t = attention_t[:width], attention_t[width:]
    queries = product(first_entry, query_t, "td,ed->te").astype(BF16)
    keys = product(group_entry, attention_t[width : 2 * width], "td,ed->te").astype(BF16)
    values = product(group_entry, attention_t[2 * width :], "td,ed->te").astype(BF16)
    mixed_heads, exact_heads, totals = attention_forward(queries, keys, values, low, high)
    attended = product(mixed_heads, projection_t, "td,ed->te").reshape(slots, IMG_SHORT, width)
    inputs = patches.astype(F32).reshape(slots, IMG_SHORT, width)
    middle = inputs + gate_a * attended
    normed_b = normalize(middle)
    second = (normed_b * (1.0 + scale_b) + shift_b).astype(BF16).reshape(local_rows, width)

    arrived = exchange(pack(places_t, None, second, capacity))
    expert_active, grad_expert_hidden, grad_sent = feed(
        arrived, grad_arrived, up, down, False, BF16, False
    )
    grad_returned = exchange(grad_sent)
    produced = product(expert_active, down, "rf,fd->rd").astype(BF16)
    returned = exchange(produced)

    activated, grad_hidden, grad_second, shared = feed(
        second, grad_shared, expand_t, contract_t, True, F32, True
    )
    contract_grad_t = product(grad_shared, activated, "td,tf->df").astype(BF16)
    expand_grad_t = product(grad_hidden, second, "tf,td->fd").astype(BF16)
    down_grad = product(expert_active, grad_arrived, "rf,rd->fd")
    up_grad = product(arrived, grad_expert_hidden, "rd,rf->df")
    expert_up_grad = reduce_narrow(up_grad, 0)[None]
    expert_down_grad = reduce_narrow(down_grad, 0)[None]

    grad_second = grad_second + combine(places, None, grad_returned, capacity)
    grad_second = grad_second.reshape(slots, IMG_SHORT, width)
    grad_shift_b = jnp.sum(grad_second, axis=1)
    grad_scale_b = jnp.sum(grad_second * normed_b, axis=1)
    grad_middle = grad_top + norm_back(middle, grad_second * (1.0 + scale_b))
    grad_gate_a = jnp.sum(grad_middle * attended, axis=1)
    grad_attended = (gate_a * grad_middle).reshape(local_rows, width).astype(BF16)
    projection_grad_t = product(grad_attended, mixed_heads, "te,td->ed").astype(BF16)
    grad_mixed = product(grad_attended, projection_t, "te,ed->td").astype(BF16)
    grad_queries, grad_keys, grad_values = attention_backward(
        queries, keys, values, grad_mixed, exact_heads, totals, low, high
    )

    mixture = shared + combine(places, gates, returned, capacity)
    mixture = mixture.reshape(slots, IMG_SHORT, width)
    block_out = (middle + gate_b * mixture).reshape(local_rows, width).astype(BF16)
    grad_gate_b = jnp.sum(grad_top * mixture, axis=1)

    attention_grad_t = jnp.concatenate(
        [
            product(grad_queries, first_entry, "te,td->ed").astype(BF16),
            product(grad_keys, group_entry, "te,td->ed").astype(BF16),
            product(grad_values, group_entry, "te,td->ed").astype(BF16),
        ],
        axis=0,
    )
    grad_group = product(grad_keys, attention_t[width : 2 * width], "te,ed->td") + product(
        grad_values, attention_t[2 * width :], "te,ed->td"
    )
    grad_entry = reduce_narrow(grad_group, 0) + product(grad_queries, query_t, "te,ed->td")
    grad_entry = grad_entry.reshape(slots, IMG_SHORT, width)
    grad_shift_a = jnp.sum(grad_entry, axis=1)
    grad_scale_a = jnp.sum(grad_entry * normalize(inputs), axis=1)
    grad_inputs = grad_middle + norm_back(inputs, grad_entry * (1.0 + scale_a))
    patch_grad = grad_inputs.reshape(local_rows, width).astype(BF16)

    grad_modulation = jnp.stack(
        [grad_shift_a, grad_scale_a, grad_gate_a, grad_shift_b, grad_scale_b, grad_gate_b], axis=1
    )
    grad_modulation = grad_modulation.reshape(slots, experts, share).astype(BF16)
    grad_modulation = lax.all_to_all(
        grad_modulation.transpose(1, 0, 2), "wide", split_axis=0, concat_axis=0, tiled=True
    )
    grad_modulation = lax.all_gather(grad_modulation, "narrow", axis=1, tiled=True)
    row_share = width // narrow
    modulation_grad = product(
        part_of(lifted, mine, row_share, 1),
        grad_modulation.reshape(experts * group_slots, share),
        "sd,se->de",
    )
    expand_grad = reduce_narrow(reduce_wide(expand_grad_t), 1).T
    contract_grad = reduce_narrow(reduce_wide(contract_grad_t), 1).T
    projection_grad = reduce_narrow(reduce_wide(projection_grad_t), 1).T
    attention_grad = reduce_narrow(reduce_wide(attention_grad_t), 1).T
    return (
        block_out,
        patch_grad,
        modulation_grad,
        attention_grad,
        projection_grad,
        expand_grad,
        contract_grad,
        expert_up_grad,
        expert_down_grad,
    )


def solution(mesh):
    rows = P(("wide", "narrow"), None)
    dense = P("narrow", "wide")
    expert = P("wide", "narrow", None)
    return jax.shard_map(
        on_device,
        mesh=mesh,
        in_specs=(rows, rows, dense, dense, dense, dense, dense, expert, expert, P("wide"), rows, rows, rows),
        out_specs=(rows, rows, dense, dense, dense, dense, dense, expert, expert),
        check_vma=False,
    )
```

```python
import functools

import jax
import jax.numpy as jnp
from jax import lax
from jax.experimental import pallas as pl
from jax.experimental.pallas import tpu as pltpu
from jax.sharding import PartitionSpec as P

HEADS = 12
IMG_SHORT = 256
EPSILON = 1e-06
QUAD = 4
HALVES = 2
FORWARD_CHUNK = 512
BACKWARD_CHUNK = 1024
FEED_ROWS = 512
FEED_TILE = 768
PACK_EXPERTS = 2
COMBINE_ROWS = 256
F32 = jnp.float32
BF16 = jnp.bfloat16
NN = (((1,), (0,)), ((), ()))
NT = (((1,), (1,)), ((), ()))
VMEM_BYTES = 48 << 20


def dot(left, right, dims=NN):
    return lax.dot_general(left, right, dims, preferred_element_type=F32)


def product(left, right, form):
    return jnp.einsum(form, left, right, preferred_element_type=F32)


def normalize(values):
    centered = values - jnp.mean(values, axis=-1, keepdims=True)
    variance = jnp.mean(centered * centered, axis=-1, keepdims=True)
    return centered * lax.rsqrt(variance + EPSILON)


def norm_back(values, grad_normed):
    centered = values - jnp.mean(values, axis=-1, keepdims=True)
    variance = jnp.mean(centered * centered, axis=-1, keepdims=True)
    inverse = lax.rsqrt(variance + EPSILON)
    normed = centered * inverse
    return inverse * (
        grad_normed
        - jnp.mean(grad_normed, axis=-1, keepdims=True)
        - normed * jnp.mean(grad_normed * normed, axis=-1, keepdims=True)
    )


def of_head(values, which, axis, head_dim):
    place = lax.broadcasted_iota(jnp.int32, values.shape, axis) // head_dim
    return jnp.where(place == which, values, jnp.zeros_like(values))


def over_keys(low, high, key_rows, chunk, step, state):
    def unrolled():
        inner = state
        for start in range(0, key_rows, chunk):
            inner = step(start, chunk, inner)
        return inner

    def looped():
        first, inner = low, state
        for count in (4, 2, 1):
            size = count * IMG_SHORT
            if size > key_rows:
                continue
            turns = (high - first) // count

            def body(index, inner, first=first, count=count, size=size):
                start = (first + index * count) * IMG_SHORT
                return step(pl.multiple_of(start, IMG_SHORT), size, inner)

            inner = lax.fori_loop(0, turns, body, inner)
            first = first + turns * count
        return inner

    return lax.cond((high - low) * IMG_SHORT == key_rows, unrolled, looped)


def forward_kernel(
    head_dim, low_ref, high_ref, q_ref, k_ref, v_ref, out_ref, exact_ref, total_ref, vt, kept
):
    row_block = pl.program_id(1)

    @pl.when(row_block == 0)
    def _():
        vt[...] = v_ref[...].T

    queries = (q_ref[...].astype(F32) * head_dim**-0.5).astype(BF16).T
    rows = q_ref.shape[0]
    by_head = [of_head(queries, h, 0, head_dim) for h in range(QUAD)]
    low, high = low_ref[row_block], high_ref[row_block]
    key_rows = k_ref.shape[0]

    def score_step(at, size, tops):
        keys = k_ref[pl.ds(at, size), :]
        fresh = []
        for h in range(QUAD):
            scores = dot(keys, by_head[h])
            kept[h, pl.ds(at, size), :] = scores
            fresh.append(
                jnp.maximum(tops[h], jnp.max(scores.reshape(size // 8, 8, rows), axis=0))
            )
        return tuple(fresh)

    chunk = min(FORWARD_CHUNK, key_rows)
    tops = over_keys(
        low, high, key_rows, chunk, score_step, tuple(jnp.full((8, rows), -1e30, F32) for _ in range(QUAD))
    )
    tops = [jnp.max(t, axis=0, keepdims=True) for t in tops]

    def mix_step(at, size, state):
        fresh = []
        for h in range(QUAD):
            total, mixed = state[h]
            weights = jnp.exp(kept[h, pl.ds(at, size), :] - tops[h])
            total = total + jnp.sum(weights.reshape(size // 8, 8, rows), axis=0)
            values = vt[h * head_dim : (h + 1) * head_dim, pl.ds(at, size)]
            fresh.append((total, mixed + dot(values, weights.astype(BF16))))
        return tuple(fresh)

    state = over_keys(
        low,
        high,
        key_rows,
        chunk,
        mix_step,
        tuple((jnp.zeros((8, rows), F32), jnp.zeros((head_dim, rows), F32)) for _ in range(QUAD)),
    )
    mixed = []
    for h in range(QUAD):
        total = jnp.sum(state[h][0], axis=0, keepdims=True)
        mixed.append(state[h][1] / total)
        total_ref[0, h : h + 1, :] = tops[h] + jnp.log(total)
    mixed = jnp.concatenate(mixed, axis=0).T
    exact_ref[...] = mixed
    out_ref[...] = mixed.astype(BF16)


def attention_forward(queries, keys, values, low, high):
    rows, width = queries.shape
    key_rows = keys.shape[0]
    head_dim = width // HEADS
    lanes, quads = QUAD * head_dim, HEADS // QUAD
    size = IMG_SHORT
    row_spec = pl.BlockSpec((size, lanes), lambda j, i, *_: (i, j))
    key_spec = pl.BlockSpec((key_rows, lanes), lambda j, i, *_: (0, j))
    return pl.pallas_call(
        functools.partial(forward_kernel, head_dim),
        grid_spec=pltpu.PrefetchScalarGridSpec(
            num_scalar_prefetch=2,
            grid=(quads, rows // size),
            in_specs=[row_spec, key_spec, key_spec],
            out_specs=[
                row_spec,
                row_spec,
                pl.BlockSpec((1, QUAD, size), lambda j, i, *_: (j, 0, i)),
            ],
            scratch_shapes=[
                pltpu.VMEM((lanes, key_rows), BF16),
                pltpu.VMEM((QUAD, key_rows, size), F32),
            ],
        ),
        out_shape=[
            jax.ShapeDtypeStruct((rows, width), BF16),
            jax.ShapeDtypeStruct((rows, width), F32),
            jax.ShapeDtypeStruct((quads, QUAD, rows), F32),
        ],
        compiler_params=pltpu.CompilerParams(vmem_limit_bytes=VMEM_BYTES),
        cost_estimate=pl.CostEstimate(
            flops=16 * rows * key_rows * width,
            transcendentals=rows * key_rows * HEADS,
            bytes_accessed=4 * key_rows * width + 8 * rows * width,
        ),
        name="attention_forward",
    )(low, high, queries, keys, values)


def backward_kernel(
    head_dim,
    low_ref,
    high_ref,
    q_ref,
    k_ref,
    v_ref,
    grad_ref,
    exact_ref,
    total_ref,
    dq_ref,
    dk_ref,
    dv_ref,
    kt,
    dk_sum,
    dv_sum,
):
    row_block = pl.program_id(1)

    @pl.when(row_block == 0)
    def _():
        kt[...] = k_ref[...].T
        dk_sum[...] = jnp.zeros_like(dk_sum)
        dv_sum[...] = jnp.zeros_like(dv_sum)

    scale = head_dim**-0.5
    queries = (q_ref[...].astype(F32) * scale).astype(BF16)
    grads = grad_ref[...]
    rows = queries.shape[0]
    heads = range(QUAD)
    dots = (grads.astype(F32) * exact_ref[...]).T
    dots = [
        jnp.sum(dots[h * head_dim : (h + 1) * head_dim], axis=0, keepdims=True) for h in heads
    ]
    q_columns, g_columns = queries.T, grads.T
    q_columns = [of_head(q_columns, h, 0, head_dim) for h in heads]
    g_columns = [of_head(g_columns, h, 0, head_dim) for h in heads]
    q_rows = jnp.concatenate([of_head(queries, h, 1, head_dim) for h in heads], axis=0)
    g_rows = jnp.concatenate([of_head(grads, h, 1, head_dim) for h in heads], axis=0)
    totals = [total_ref[0, h : h + 1, :] for h in heads]
    low, high = low_ref[row_block], high_ref[row_block]
    key_rows = k_ref.shape[0]

    def step(at, size, dq):
        keys = k_ref[pl.ds(at, size), :]
        values = v_ref[pl.ds(at, size), :]
        weights, score_grads, fresh = [], [], []
        for h in heads:
            softmax = jnp.exp(dot(keys, q_columns[h]) - totals[h])
            grad = (softmax * (dot(values, g_columns[h]) - dots[h])).astype(BF16)
            weights.append(softmax.astype(BF16))
            score_grads.append(grad)
            columns = kt[h * head_dim : (h + 1) * head_dim, pl.ds(at, size)]
            fresh.append(dq[h] + dot(columns, grad))
        dv_sum[pl.ds(at, size), :] += dot(jnp.concatenate(weights, axis=1), g_rows)
        dk_sum[pl.ds(at, size), :] += dot(jnp.concatenate(score_grads, axis=1), q_rows)
        return tuple(fresh)

    chunk = min(BACKWARD_CHUNK, key_rows)
    dq = over_keys(
        low, high, key_rows, chunk, step, tuple(jnp.zeros((head_dim, rows), F32) for _ in heads)
    )
    dq_ref[...] = (jnp.concatenate(dq, axis=0) * scale).T.astype(BF16)

    @pl.when(row_block == pl.num_programs(1) - 1)
    def _():
        dk_ref[...] = dk_sum[...].astype(BF16)
        dv_ref[...] = dv_sum[...].astype(BF16)


def attention_backward(queries, keys, values, grads, exact, totals, low, high):
    rows, width = queries.shape
    key_rows = keys.shape[0]
    head_dim = width // HEADS
    lanes, quads = QUAD * head_dim, HEADS // QUAD
    size = IMG_SHORT
    row_spec = pl.BlockSpec((size, lanes), lambda j, i, *_: (i, j))
    key_spec = pl.BlockSpec((key_rows, lanes), lambda j, i, *_: (0, j))
    return pl.pallas_call(
        functools.partial(backward_kernel, head_dim),
        grid_spec=pltpu.PrefetchScalarGridSpec(
            num_scalar_prefetch=2,
            grid=(quads, rows // size),
            in_specs=[
                row_spec,
                key_spec,
                key_spec,
                row_spec,
                row_spec,
                pl.BlockSpec((1, QUAD, size), lambda j, i, *_: (j, 0, i)),
            ],
            out_specs=[row_spec, key_spec, key_spec],
            scratch_shapes=[
                pltpu.VMEM((lanes, key_rows), BF16),
                pltpu.VMEM((key_rows, lanes), F32),
                pltpu.VMEM((key_rows, lanes), F32),
            ],
        ),
        out_shape=[
            jax.ShapeDtypeStruct((rows, width), BF16),
            jax.ShapeDtypeStruct((key_rows, width), BF16),
            jax.ShapeDtypeStruct((key_rows, width), BF16),
        ],
        compiler_params=pltpu.CompilerParams(vmem_limit_bytes=VMEM_BYTES),
        cost_estimate=pl.CostEstimate(
            flops=40 * rows * key_rows * width,
            transcendentals=rows * key_rows * HEADS,
            bytes_accessed=8 * key_rows * width + 10 * rows * width,
        ),
        name="attention_backward",
    )(low, high, queries, keys, values, grads, exact, totals)


def pack_kernel(count, place_ref, scale_ref, values_ref, *outs):
    half = outs[0].shape[0] // count
    capacity = half * len(outs)
    picks, scales = [], []
    for index in range(count):
        expert = pl.program_id(0) * count + index
        places = place_ref[pl.ds(expert, 1), :]
        slots = lax.broadcasted_iota(jnp.int32, (capacity, places.shape[1]), 0)
        chosen = slots == places
        picks.append(chosen.astype(BF16))
        if scale_ref is not None:
            scale = jnp.where(chosen, scale_ref[pl.ds(expert, 1), :], 0.0)
            scales.append(jnp.sum(scale, axis=1, keepdims=True))
    rows = dot(jnp.concatenate(picks, axis=0), values_ref[...])
    if scale_ref is not None:
        rows = rows * jnp.concatenate(scales, axis=0)
    for index in range(count):
        for which, out_ref in enumerate(outs):
            start = index * capacity + which * half
            part = rows[start : start + half]
            out_ref[index * half : (index + 1) * half, :] = part.astype(BF16)


def pack(places, scales, values, capacity):
    experts, rows = places.shape
    width = values.shape[1]
    half = capacity // HALVES
    whole = lambda shape: pl.BlockSpec(shape, lambda e: (0, 0))
    operands = [places, values] if scales is None else [places, scales, values]
    count = min(PACK_EXPERTS, experts)
    kernel = functools.partial(pack_kernel, count)
    if scales is None:
        kernel = lambda place_ref, values_ref, *outs: pack_kernel(
            count, place_ref, None, values_ref, *outs
        )
    return pl.pallas_call(
        kernel,
        grid=(experts // count,),
        in_specs=[whole(o.shape) for o in operands],
        out_specs=[pl.BlockSpec((count * half, width), lambda e: (e, 0))] * HALVES,
        out_shape=[jax.ShapeDtypeStruct((experts * half, width), BF16)] * HALVES,
        compiler_params=pltpu.CompilerParams(vmem_limit_bytes=VMEM_BYTES),
        cost_estimate=pl.CostEstimate(
            flops=2 * experts * capacity * rows * width,
            transcendentals=0,
            bytes_accessed=2 * width * (rows + experts * capacity),
        ),
        name="pack",
    )(*operands)


def combine_kernel(experts, capacity, place_ref, scale_ref, first_ref, second_ref, out_ref):
    half = capacity // HALVES
    total = None
    tokens = out_ref.shape[0]
    slots = lax.broadcasted_iota(jnp.int32, (tokens, capacity), 1)
    for expert in range(experts):
        scale = 1.0 if scale_ref is None else scale_ref[:, expert : expert + 1]
        chosen = jnp.where(slots == place_ref[:, expert : expert + 1], scale, 0.0)
        span = slice(expert * half, (expert + 1) * half)
        rows = jnp.concatenate([first_ref[span, :], second_ref[span, :]], axis=0)
        part = dot(chosen.astype(BF16), rows)
        total = part if total is None else total + part
    out_ref[...] = total


def combine(places, scales, rows, capacity):
    tokens, experts = places.shape
    width = rows[0].shape[1]
    block = min(COMBINE_ROWS, tokens)
    part = pl.BlockSpec((block, experts), lambda i: (i, 0))
    kernel = functools.partial(combine_kernel, experts, capacity)
    operands = [places] if scales is None else [places, scales]
    if scales is None:
        kernel = lambda place_ref, *refs: combine_kernel(
            experts, capacity, place_ref, None, *refs
        )
    return pl.pallas_call(
        kernel,
        grid=(tokens // block,),
        in_specs=[part] * len(operands)
        + [pl.BlockSpec(r.shape, lambda i: (0, 0), pipeline_mode=pl.Buffered(1)) for r in rows],
        out_specs=pl.BlockSpec((block, width), lambda i: (i, 0)),
        out_shape=jax.ShapeDtypeStruct((tokens, width), F32),
        compiler_params=pltpu.CompilerParams(vmem_limit_bytes=VMEM_BYTES),
        cost_estimate=pl.CostEstimate(
            flops=2 * experts * capacity * tokens * width,
            transcendentals=0,
            bytes_accessed=2 * width * (2 * tokens + experts * capacity),
        ),
        name="combine",
    )(*operands, *rows)


def gelu_both(hidden):
    inner = 0.7978845608028654
    square = hidden * hidden
    bend = jnp.tanh(hidden * (inner + (inner * 0.044715) * square))
    half = 0.5 + 0.5 * bend
    slope = half + (0.5 * hidden) * (1.0 - bend * bend) * (inner + (3 * inner * 0.044715) * square)
    return hidden * half, slope


def feed_kernel(
    transposed, tile, with_out, in_ref, grad_ref, up_ref, down_ref, act_ref, hid_ref, back_ref, *out
):
    rows, grads = in_ref[...], grad_ref[...]
    hidden_size = act_ref.shape[1]
    for start in range(0, hidden_size, tile):
        part = slice(start, start + tile)
        if transposed:
            hidden = dot(rows, up_ref[part, :], NT)
            grad = dot(grads, down_ref[start // tile])
        else:
            hidden = dot(rows, up_ref[:, part])
            grad = dot(grads, down_ref[part, :], NT)
        active, slope = gelu_both(hidden)
        act_ref[:, part] = active.astype(BF16)
        hid_ref[:, part] = (grad * slope).astype(BF16)
    back = dot(hid_ref[...], up_ref[...], NN if transposed else NT)
    back_ref[...] = back.astype(back_ref.dtype)
    if with_out and not transposed:
        out[0][...] = dot(act_ref[...], down_ref[...]).astype(out[0].dtype)
    if with_out and transposed:
        made = [
            dot(act_ref[:, p * tile : (p + 1) * tile], down_ref[p], NT)
            for p in range(hidden_size // tile)
        ]
        out[0][...] = sum(made).astype(out[0].dtype)


def feed(rows, grads, up, down, transposed, out_dtype, with_out):
    count, width = rows.shape
    hidden_size = up.shape[0] if transposed else up.shape[1]
    block = min(FEED_ROWS, count)
    row = pl.BlockSpec((block, width), lambda i: (i, 0))
    hid = pl.BlockSpec((block, hidden_size), lambda i: (i, 0))
    fixed = lambda a: pl.BlockSpec(a.shape, lambda i: (0,) * a.ndim, pipeline_mode=pl.Buffered(1))
    tile = width if transposed else min(FEED_TILE, hidden_size)
    extra = 1 if with_out else 0
    return pl.pallas_call(
        functools.partial(feed_kernel, transposed, tile, with_out),
        grid=(count // block,),
        in_specs=[row, row, fixed(up), fixed(down)],
        out_specs=[hid, hid, row] + [row] * extra,
        out_shape=[
            jax.ShapeDtypeStruct((count, hidden_size), BF16),
            jax.ShapeDtypeStruct((count, hidden_size), BF16),
            jax.ShapeDtypeStruct((count, width), out_dtype),
        ]
        + [jax.ShapeDtypeStruct((count, width), out_dtype)] * extra,
        compiler_params=pltpu.CompilerParams(vmem_limit_bytes=VMEM_BYTES),
        cost_estimate=pl.CostEstimate(
            flops=(6 + 2 * extra) * count * width * hidden_size,
            transcendentals=count * hidden_size,
            bytes_accessed=4 * count * hidden_size + 8 * count * width + 4 * width * hidden_size,
        ),
        name="feed",
    )(rows, grads, up, down)


def swap(values):
    return lax.ppermute(values, "narrow", [(0, 1), (1, 0)])


def other_narrow(values):
    if lax.axis_size("narrow") != 2:
        return lax.all_gather(values, "narrow", axis=0, tiled=False)
    return swap(values)


def merge_narrow(values, other, axis):
    if lax.axis_size("narrow") != 2:
        return jnp.concatenate([other[i] for i in range(other.shape[0])], axis=axis)
    return jnp.where(
        lax.axis_index("narrow") == 0,
        jnp.concatenate([values, other], axis=axis),
        jnp.concatenate([other, values], axis=axis),
    )


def gather_narrow(values, axis):
    return merge_narrow(values, other_narrow(values), axis)


def part_of(values, index, size, axis):
    return lax.dynamic_slice_in_dim(values, index * size, size, axis)


def reduce_narrow(values, axis):
    count = lax.axis_size("narrow")
    if count != 2:
        return lax.psum_scatter(
            values.astype(BF16), "narrow", scatter_dimension=axis, tiled=True
        ).astype(F32)
    size = values.shape[axis] // 2
    index = lax.axis_index("narrow")
    other = swap(part_of(values, 1 - index, size, axis).astype(BF16))
    return part_of(values, index, size, axis).astype(F32) + other.astype(F32)


def together(*values):
    return lax.optimization_barrier(values)


def to_all(blocks):
    return lax.all_to_all(blocks, "wide", split_axis=0, concat_axis=0, tiled=True)


def exchange(rows):
    wide = lax.axis_size("wide")
    blocks = rows.reshape(wide, rows.shape[0] // wide, rows.shape[1])
    return to_all(blocks).reshape(rows.shape)


def add_narrow(values, other):
    if lax.axis_size("narrow") != 2:
        return reduce_narrow(values, 0)
    own = part_of(values, lax.axis_index("narrow"), other.shape[0], 0)
    return own.astype(F32) + other.astype(F32)


def join_halves(first, second, experts):
    width = first.shape[1]
    parts = [h.reshape(experts, -1, width) for h in (first, second)]
    return jnp.concatenate(parts, axis=1).reshape(-1, width)


def split_halves(rows, experts):
    width = rows.shape[1]
    parts = jnp.split(rows.reshape(experts, -1, width), 2, axis=1)
    return [p.reshape(-1, width) for p in parts]


def gather_wide(values):
    return lax.all_gather(values, "wide", axis=0, tiled=True)


def reduce_wide(values):
    return lax.psum_scatter(values, "wide", scatter_dimension=0, tiled=True)


def on_device(
    patches,
    conditions,
    modulation_weight,
    attention_weight,
    projection_weight,
    expand_weight,
    contract_weight,
    expert_expand,
    expert_contract,
    image_start,
    routes,
    route_gates,
    cotangent,
):
    local_rows, width = patches.shape
    slots = conditions.shape[0]
    experts = lax.axis_size("wide")
    narrow = lax.axis_size("narrow")
    capacity = 4 * local_rows // experts
    mine = lax.axis_index("narrow")
    group_slots = narrow * slots
    group_rows = narrow * local_rows

    modulation_columns = gather_narrow(modulation_weight, 0)
    spread = jnp.broadcast_to(conditions[None], (experts, slots, width))
    all_conditions = gather_narrow(to_all(spread)[:, None], 1).reshape(-1, width)
    rows_shard = gather_narrow(
        jnp.concatenate([attention_weight.T, projection_weight.T, expand_weight.T], axis=0), 1
    )
    contract_shard = gather_narrow(contract_weight.T, 1)
    column_share, hidden_size = contract_shard.shape
    half = width // narrow
    pieces = hidden_size // width
    contract_shard = contract_shard.reshape(column_share, pieces, width).transpose(1, 0, 2)
    contract_shard = contract_shard.reshape(pieces * column_share, width)
    dense_shard = jnp.concatenate([rows_shard, contract_shard], axis=0)
    dense = gather_wide(dense_shard)
    dense = dense.reshape(experts, -1, width)
    expand_end = rows_shard.shape[0]
    attention_end = attention_weight.shape[1]
    projection_end = attention_end + column_share
    attention_t = dense[:, :attention_end].reshape(3 * width, width)
    projection_t = dense[:, attention_end:projection_end].reshape(width, width)
    expand_t = dense[:, projection_end:expand_end].reshape(hidden_size, width)
    contract_t = dense[:, expand_end:].reshape(experts, pieces, column_share, width)
    contract_t = contract_t.transpose(1, 0, 2, 3).reshape(pieces, width, width)
    ready_patches, all_conditions, modulation_columns = together(
        patches, all_conditions, modulation_columns
    )
    group_patches = gather_narrow(ready_patches, 0)
    ready_up, ready_down, group_patches = together(
        expert_expand[0], expert_contract[0], group_patches
    )
    other_up, other_down = other_narrow(ready_up), other_narrow(ready_down)

    lifted = jax.nn.silu(all_conditions.astype(F32)).astype(BF16)
    columns = jnp.dot(lifted, modulation_columns, preferred_element_type=F32)
    share = columns.shape[1]
    modulation = to_all(columns.reshape(experts, group_slots, share))
    modulation = modulation.transpose(1, 0, 2).reshape(group_slots, 6, 1, width)
    own = part_of(modulation, mine, slots, 0)
    shift_a, scale_a, gate_a, shift_b, scale_b, gate_b = [own[:, i] for i in range(6)]

    expert_ids = jnp.arange(experts, dtype=jnp.int32)[None, :]
    named = routes[:, :, None] == expert_ids[None]
    chosen = jnp.any(named, axis=1)
    order = jnp.arange(local_rows, dtype=jnp.int32)
    earlier = (order[:, None] > order[None, :]).astype(BF16)
    rank = jnp.dot(earlier, chosen.astype(BF16), preferred_element_type=F32).astype(jnp.int32)
    places = jnp.where(chosen, rank, -1)
    gates = jnp.sum(jnp.where(named, route_gates[:, :, None], 0.0), axis=1)
    places_t, gates_t = places.T, gates.T

    grad_top = cotangent.astype(F32).reshape(slots, IMG_SHORT, width)
    grad_shared = (gate_b * grad_top).astype(BF16).reshape(local_rows, width)
    grad_packed = pack(places_t, gates_t, grad_shared, capacity)
    grad_first, attention_t = together(grad_packed[0], attention_t)
    grad_arrived = [exchange(grad_first)]

    block_start = image_start.reshape(group_slots, IMG_SHORT)[:, 0]
    own_start = part_of(block_start, mine, slots, 0)
    low = own_start - block_start[0]
    high = low + jnp.sum(own_start[:, None] == block_start[None, :], axis=1, dtype=jnp.int32)
    group_inputs = group_patches.astype(F32).reshape(group_slots, IMG_SHORT, width)
    group_entry = (
        (normalize(group_inputs) * (1.0 + modulation[:, 1]) + modulation[:, 0])
        .astype(BF16)
        .reshape(group_rows, width)
    )
    first_entry = part_of(group_entry, mine, local_rows, 0)
    query_t, key_value_t = attention_t[:width], attention_t[width:]
    queries = product(first_entry, query_t, "td,ed->te").astype(BF16)
    keys = product(group_entry, attention_t[width : 2 * width], "td,ed->te").astype(BF16)
    values = product(group_entry, attention_t[2 * width :], "td,ed->te").astype(BF16)
    mixed_heads, exact_heads, totals = attention_forward(queries, keys, values, low, high)
    grad_last, mixed_heads, grad_arrived[0], other_down = together(
        grad_packed[1], mixed_heads, grad_arrived[0], other_down
    )
    grad_arrived.append(exchange(grad_last))
    attended = product(mixed_heads, projection_t, "td,ed->te").reshape(slots, IMG_SHORT, width)
    inputs = patches.astype(F32).reshape(slots, IMG_SHORT, width)
    middle = inputs + gate_a * attended
    normed_b = normalize(middle)
    second = (normed_b * (1.0 + scale_b) + shift_b).astype(BF16).reshape(local_rows, width)

    packed = list(pack(places_t, None, second, capacity))
    packed[0], grad_arrived[1], other_up = together(packed[0], grad_arrived[1], other_up)
    arrived = [exchange(packed[0])]
    activated, grad_hidden, grad_second, shared = feed(
        second, grad_shared, expand_t, contract_t, True, F32, True
    )
    up = merge_narrow(expert_expand[0], other_up, 0)
    down = merge_narrow(expert_contract[0], other_down, 0)
    last_packed, grad_second, up, down, arrived[0] = together(
        packed[1], grad_second, up, down, arrived[0]
    )
    arrived.append(exchange(last_packed))
    fed = feed(arrived[0], grad_arrived[0], up, down, False, BF16, True)
    grad_ready, arrived[1] = together(fed[2], arrived[1])
    grad_returned = [exchange(grad_ready)]
    fed_last = feed(arrived[1], grad_arrived[1], up, down, False, BF16, True)
    grad_ready, grad_returned[0] = together(fed_last[2], grad_returned[0])
    grad_returned.append(exchange(grad_ready))
    expert_active, grad_expert_hidden = (fed[0], fed_last[0]), (fed[1], fed_last[1])
    spans = [slice(i * half, (i + 1) * half) for i in range(hidden_size // half)]
    contract_grads = [
        product(grad_shared, activated[:, span], "td,tf->df")
        .astype(BF16)
        .reshape(experts, column_share, half)
        for span in spans
    ]
    expand_grads = [
        product(grad_hidden, second[:, span], "tf,td->fd").astype(BF16).reshape(experts, -1, half)
        for span in spans[:narrow]
    ]
    folds = len(spans) // narrow
    shared_grads = jnp.stack(
        [
            jnp.concatenate(
                [expand_grads[i], *contract_grads[i * folds : (i + 1) * folds]], axis=1
            )
            for i in range(narrow)
        ]
    )
    shared_grads = shared_grads.reshape(narrow, -1, half)
    other_shared = swap(part_of(shared_grads, 1 - mine, 1, 0)) if narrow == 2 else shared_grads
    produced = join_halves(fed[3], fed_last[3], experts)
    down_grad = sum(product(a, g, "rf,rd->fd") for a, g in zip(expert_active, grad_arrived))
    up_grad = sum(product(a, g, "rd,rf->df") for a, g in zip(arrived, grad_expert_hidden))
    send_up = part_of(up_grad, 1 - mine, half, 0) if narrow == 2 else up_grad
    send_down = part_of(down_grad, 1 - mine, hidden_size // 2, 0) if narrow == 2 else down_grad
    *grad_returned, send_up, send_down, produced, other_shared = together(
        *grad_returned, send_up.astype(BF16), send_down.astype(BF16), produced, other_shared
    )
    returned = produced
    returned = exchange(returned)

    shared_sum = reduce_wide(add_narrow(shared_grads, other_shared)[0].astype(BF16))
    other_up_grad = swap(send_up) if narrow == 2 else send_up
    other_down_grad = swap(send_down) if narrow == 2 else send_down

    grad_second = grad_second + combine(places, None, grad_returned, capacity)
    grad_second = grad_second.reshape(slots, IMG_SHORT, width)
    grad_shift_b = jnp.sum(grad_second, axis=1)
    grad_scale_b = jnp.sum(grad_second * normed_b, axis=1)
    grad_middle = grad_top + norm_back(middle, grad_second * (1.0 + scale_b))
    grad_gate_a = jnp.sum(grad_middle * attended, axis=1)
    grad_attended = (gate_a * grad_middle).reshape(local_rows, width).astype(BF16)
    projection_grad_t = product(grad_attended, mixed_heads, "te,td->ed").astype(BF16)
    grad_mixed = product(grad_attended, projection_t, "te,ed->td").astype(BF16)
    grad_queries, grad_keys, grad_values = attention_backward(
        queries, keys, values, grad_mixed, exact_heads, totals, low, high
    )

    returned = together(returned, grad_queries)[0]
    other_up_grad, other_down_grad, grad_queries, grad_keys, grad_values = together(
        other_up_grad, other_down_grad, grad_queries, grad_keys, grad_values
    )
    expert_up_grad = add_narrow(up_grad, other_up_grad)[None]
    expert_down_grad = add_narrow(down_grad, other_down_grad)[None]
    returned = split_halves(returned, experts)
    mixture = shared + combine(places, gates, returned, capacity)
    mixture = mixture.reshape(slots, IMG_SHORT, width)
    grad_group = product(grad_keys, attention_t[width : 2 * width], "te,ed->td") + product(
        grad_values, attention_t[2 * width :], "te,ed->td"
    )
    grad_own = product(grad_queries, query_t, "te,ed->td")
    if narrow == 2:
        other_entry = swap(part_of(grad_group, 1 - mine, local_rows, 0).astype(BF16))
        other_entry, mixture = together(other_entry, mixture)
        grad_entry = add_narrow(grad_group, other_entry) + grad_own
    else:
        grad_entry = reduce_narrow(grad_group, 0) + grad_own
    attention_grad_t = jnp.concatenate(
        [
            product(grad_queries, first_entry, "te,td->ed").astype(BF16),
            product(grad_keys, group_entry, "te,td->ed").astype(BF16),
            product(grad_values, group_entry, "te,td->ed").astype(BF16),
        ],
        axis=0,
    )
    block_out = (middle + gate_b * mixture).reshape(local_rows, width).astype(BF16)
    grad_gate_b = jnp.sum(grad_top * mixture, axis=1)
    grad_entry = grad_entry.reshape(slots, IMG_SHORT, width)
    grad_shift_a = jnp.sum(grad_entry, axis=1)
    grad_scale_a = jnp.sum(grad_entry * normalize(inputs), axis=1)
    grad_inputs = grad_middle + norm_back(inputs, grad_entry * (1.0 + scale_a))
    patch_grad = grad_inputs.reshape(local_rows, width).astype(BF16)

    grad_modulation = jnp.stack(
        [grad_shift_a, grad_scale_a, grad_gate_a, grad_shift_b, grad_scale_b, grad_gate_b], axis=1
    )
    grad_modulation = grad_modulation.reshape(slots, experts, share).astype(BF16)
    grad_modulation = gather_narrow(to_all(grad_modulation.transpose(1, 0, 2))[:, None], 1)
    row_share = width // narrow
    modulation_grad = product(
        part_of(lifted, mine, row_share, 1),
        grad_modulation.reshape(experts * group_slots, share),
        "sd,se->de",
    )
    expand_share = expand_weight.shape[1]
    expand_share = expand_weight.shape[1]
    expand_grad = shared_sum[:expand_share].astype(F32).T
    contract_grad = shared_sum[expand_share:].astype(F32).reshape(folds, column_share, half)
    contract_grad = contract_grad.transpose(0, 2, 1).reshape(folds * half, column_share)
    late_grads = jnp.concatenate(
        [
            attention_grad_t.reshape(experts, attention_end, width),
            projection_grad_t.reshape(experts, column_share, width),
        ],
        axis=1,
    )
    late_sum = reduce_wide(late_grads.reshape(-1, width))
    late_sum, block_out, patch_grad, modulation_grad, expand_grad, contract_grad = together(
        late_sum, block_out, patch_grad, modulation_grad, expand_grad, contract_grad
    )
    late_sum = reduce_narrow(late_sum, 1).T
    attention_grad, projection_grad = late_sum[:, :attention_end], late_sum[:, attention_end:]
    return (
        block_out,
        patch_grad,
        modulation_grad,
        attention_grad,
        projection_grad,
        expand_grad,
        contract_grad,
        expert_up_grad,
        expert_down_grad,
    )


def solution(mesh):
    rows = P(("wide", "narrow"), None)
    dense = P("narrow", "wide")
    expert = P("wide", "narrow", None)
    return jax.shard_map(
        on_device,
        mesh=mesh,
        in_specs=(rows, rows, dense, dense, dense, dense, dense, expert, expert, P("wide"), rows, rows, rows),
        out_specs=(rows, rows, dense, dense, dense, dense, dense, expert, expert),
        check_vma=False,
    )
```

```python
import functools

import jax
import jax.numpy as jnp
from jax import lax
from jax.experimental import pallas as pl
from jax.experimental.pallas import tpu as pltpu
from jax.sharding import PartitionSpec as P

HEADS = 12
IMG_SHORT = 256
EPSILON = 1e-06
QUAD = 4
HALVES = 2
FORWARD_CHUNK = 512
BACKWARD_CHUNK = 1024
FEED_ROWS = 512
FEED_TILE = 768
PACK_EXPERTS = 2
COMBINE_ROWS = 256
F32 = jnp.float32
BF16 = jnp.bfloat16
NN = (((1,), (0,)), ((), ()))
NT = (((1,), (1,)), ((), ()))
VMEM_BYTES = 48 << 20


def dot(left, right, dims=NN):
    return lax.dot_general(left, right, dims, preferred_element_type=F32)


def product(left, right, form):
    return jnp.einsum(form, left, right, preferred_element_type=F32)


def normalize(values):
    centered = values - jnp.mean(values, axis=-1, keepdims=True)
    variance = jnp.mean(centered * centered, axis=-1, keepdims=True)
    return centered * lax.rsqrt(variance + EPSILON)


def norm_back(values, grad_normed):
    centered = values - jnp.mean(values, axis=-1, keepdims=True)
    variance = jnp.mean(centered * centered, axis=-1, keepdims=True)
    inverse = lax.rsqrt(variance + EPSILON)
    normed = centered * inverse
    return inverse * (
        grad_normed
        - jnp.mean(grad_normed, axis=-1, keepdims=True)
        - normed * jnp.mean(grad_normed * normed, axis=-1, keepdims=True)
    )


def of_head(values, which, axis, head_dim):
    place = lax.broadcasted_iota(jnp.int32, values.shape, axis) // head_dim
    return jnp.where(place == which, values, jnp.zeros_like(values))


def over_keys(low, high, key_rows, chunk, step, state):
    def unrolled():
        inner = state
        for start in range(0, key_rows, chunk):
            inner = step(start, chunk, inner)
        return inner

    def looped():
        first, inner = low, state
        for count in (4, 2, 1):
            size = count * IMG_SHORT
            if size > key_rows:
                continue
            turns = (high - first) // count

            def body(index, inner, first=first, count=count, size=size):
                start = (first + index * count) * IMG_SHORT
                return step(pl.multiple_of(start, IMG_SHORT), size, inner)

            inner = lax.fori_loop(0, turns, body, inner)
            first = first + turns * count
        return inner

    return lax.cond((high - low) * IMG_SHORT == key_rows, unrolled, looped)


def forward_kernel(
    head_dim, low_ref, high_ref, q_ref, k_ref, v_ref, out_ref, exact_ref, total_ref, vt, kept
):
    row_block = pl.program_id(1)

    @pl.when(row_block == 0)
    def _():
        vt[...] = v_ref[...].T

    queries = (q_ref[...].astype(F32) * head_dim**-0.5).astype(BF16).T
    rows = q_ref.shape[0]
    by_head = [of_head(queries, h, 0, head_dim) for h in range(QUAD)]
    low, high = low_ref[row_block], high_ref[row_block]
    key_rows = k_ref.shape[0]

    def score_step(at, size, tops):
        keys = k_ref[pl.ds(at, size), :]
        fresh = []
        for h in range(QUAD):
            scores = dot(keys, by_head[h])
            kept[h, pl.ds(at, size), :] = scores
            fresh.append(
                jnp.maximum(tops[h], jnp.max(scores.reshape(size // 8, 8, rows), axis=0))
            )
        return tuple(fresh)

    chunk = min(FORWARD_CHUNK, key_rows)
    tops = over_keys(
        low, high, key_rows, chunk, score_step, tuple(jnp.full((8, rows), -1e30, F32) for _ in range(QUAD))
    )
    tops = [jnp.max(t, axis=0, keepdims=True) for t in tops]

    def mix_step(at, size, state):
        fresh = []
        for h in range(QUAD):
            total, mixed = state[h]
            weights = jnp.exp(kept[h, pl.ds(at, size), :] - tops[h])
            total = total + jnp.sum(weights.reshape(size // 8, 8, rows), axis=0)
            values = vt[h * head_dim : (h + 1) * head_dim, pl.ds(at, size)]
            fresh.append((total, mixed + dot(values, weights.astype(BF16))))
        return tuple(fresh)

    state = over_keys(
        low,
        high,
        key_rows,
        chunk,
        mix_step,
        tuple((jnp.zeros((8, rows), F32), jnp.zeros((head_dim, rows), F32)) for _ in range(QUAD)),
    )
    mixed = []
    for h in range(QUAD):
        total = jnp.sum(state[h][0], axis=0, keepdims=True)
        mixed.append(state[h][1] / total)
        total_ref[0, h : h + 1, :] = tops[h] + jnp.log(total)
    mixed = jnp.concatenate(mixed, axis=0).T
    exact_ref[...] = mixed
    out_ref[...] = mixed.astype(BF16)


def attention_forward(queries, keys, values, low, high):
    rows, width = queries.shape
    key_rows = keys.shape[0]
    head_dim = width // HEADS
    lanes, quads = QUAD * head_dim, HEADS // QUAD
    size = IMG_SHORT
    row_spec = pl.BlockSpec((size, lanes), lambda j, i, *_: (i, j))
    key_spec = pl.BlockSpec((key_rows, lanes), lambda j, i, *_: (0, j))
    return pl.pallas_call(
        functools.partial(forward_kernel, head_dim),
        grid_spec=pltpu.PrefetchScalarGridSpec(
            num_scalar_prefetch=2,
            grid=(quads, rows // size),
            in_specs=[row_spec, key_spec, key_spec],
            out_specs=[
                row_spec,
                row_spec,
                pl.BlockSpec((1, QUAD, size), lambda j, i, *_: (j, 0, i)),
            ],
            scratch_shapes=[
                pltpu.VMEM((lanes, key_rows), BF16),
                pltpu.VMEM((QUAD, key_rows, size), F32),
            ],
        ),
        out_shape=[
            jax.ShapeDtypeStruct((rows, width), BF16),
            jax.ShapeDtypeStruct((rows, width), F32),
            jax.ShapeDtypeStruct((quads, QUAD, rows), F32),
        ],
        compiler_params=pltpu.CompilerParams(vmem_limit_bytes=VMEM_BYTES),
        cost_estimate=pl.CostEstimate(
            flops=16 * rows * key_rows * width,
            transcendentals=rows * key_rows * HEADS,
            bytes_accessed=4 * key_rows * width + 8 * rows * width,
        ),
        name="attention_forward",
    )(low, high, queries, keys, values)


def backward_kernel(
    head_dim,
    low_ref,
    high_ref,
    q_ref,
    k_ref,
    v_ref,
    grad_ref,
    exact_ref,
    total_ref,
    dq_ref,
    dk_ref,
    dv_ref,
    kt,
    dk_sum,
    dv_sum,
):
    row_block = pl.program_id(1)

    @pl.when(row_block == 0)
    def _():
        kt[...] = k_ref[...].T
        dk_sum[...] = jnp.zeros_like(dk_sum)
        dv_sum[...] = jnp.zeros_like(dv_sum)

    scale = head_dim**-0.5
    queries = (q_ref[...].astype(F32) * scale).astype(BF16)
    grads = grad_ref[...]
    rows = queries.shape[0]
    heads = range(QUAD)
    dots = (grads.astype(F32) * exact_ref[...]).T
    dots = [
        jnp.sum(dots[h * head_dim : (h + 1) * head_dim], axis=0, keepdims=True) for h in heads
    ]
    q_columns, g_columns = queries.T, grads.T
    q_columns = [of_head(q_columns, h, 0, head_dim) for h in heads]
    g_columns = [of_head(g_columns, h, 0, head_dim) for h in heads]
    q_rows = jnp.concatenate([of_head(queries, h, 1, head_dim) for h in heads], axis=0)
    g_rows = jnp.concatenate([of_head(grads, h, 1, head_dim) for h in heads], axis=0)
    totals = [total_ref[0, h : h + 1, :] for h in heads]
    low, high = low_ref[row_block], high_ref[row_block]
    key_rows = k_ref.shape[0]

    def step(at, size, dq):
        keys = k_ref[pl.ds(at, size), :]
        values = v_ref[pl.ds(at, size), :]
        weights, score_grads, fresh = [], [], []
        for h in heads:
            softmax = jnp.exp(dot(keys, q_columns[h]) - totals[h])
            grad = (softmax * (dot(values, g_columns[h]) - dots[h])).astype(BF16)
            weights.append(softmax.astype(BF16))
            score_grads.append(grad)
            columns = kt[h * head_dim : (h + 1) * head_dim, pl.ds(at, size)]
            fresh.append(dq[h] + dot(columns, grad))
        dv_sum[pl.ds(at, size), :] += dot(jnp.concatenate(weights, axis=1), g_rows)
        dk_sum[pl.ds(at, size), :] += dot(jnp.concatenate(score_grads, axis=1), q_rows)
        return tuple(fresh)

    chunk = min(BACKWARD_CHUNK, key_rows)
    dq = over_keys(
        low, high, key_rows, chunk, step, tuple(jnp.zeros((head_dim, rows), F32) for _ in heads)
    )
    dq_ref[...] = (jnp.concatenate(dq, axis=0) * scale).T.astype(BF16)

    @pl.when(row_block == pl.num_programs(1) - 1)
    def _():
        dk_ref[...] = dk_sum[...].astype(BF16)
        dv_ref[...] = dv_sum[...].astype(BF16)


def attention_backward(queries, keys, values, grads, exact, totals, low, high):
    rows, width = queries.shape
    key_rows = keys.shape[0]
    head_dim = width // HEADS
    lanes, quads = QUAD * head_dim, HEADS // QUAD
    size = IMG_SHORT
    row_spec = pl.BlockSpec((size, lanes), lambda j, i, *_: (i, j))
    key_spec = pl.BlockSpec((key_rows, lanes), lambda j, i, *_: (0, j))
    return pl.pallas_call(
        functools.partial(backward_kernel, head_dim),
        grid_spec=pltpu.PrefetchScalarGridSpec(
            num_scalar_prefetch=2,
            grid=(quads, rows // size),
            in_specs=[
                row_spec,
                key_spec,
                key_spec,
                row_spec,
                row_spec,
                pl.BlockSpec((1, QUAD, size), lambda j, i, *_: (j, 0, i)),
            ],
            out_specs=[row_spec, key_spec, key_spec],
            scratch_shapes=[
                pltpu.VMEM((lanes, key_rows), BF16),
                pltpu.VMEM((key_rows, lanes), F32),
                pltpu.VMEM((key_rows, lanes), F32),
            ],
        ),
        out_shape=[
            jax.ShapeDtypeStruct((rows, width), BF16),
            jax.ShapeDtypeStruct((key_rows, width), BF16),
            jax.ShapeDtypeStruct((key_rows, width), BF16),
        ],
        compiler_params=pltpu.CompilerParams(vmem_limit_bytes=VMEM_BYTES),
        cost_estimate=pl.CostEstimate(
            flops=40 * rows * key_rows * width,
            transcendentals=rows * key_rows * HEADS,
            bytes_accessed=8 * key_rows * width + 10 * rows * width,
        ),
        name="attention_backward",
    )(low, high, queries, keys, values, grads, exact, totals)


def pack_kernel(count, place_ref, scale_ref, values_ref, *outs):
    half = outs[0].shape[0] // count
    capacity = half * len(outs)
    picks, scales = [], []
    for index in range(count):
        expert = pl.program_id(0) * count + index
        places = place_ref[pl.ds(expert, 1), :]
        slots = lax.broadcasted_iota(jnp.int32, (capacity, places.shape[1]), 0)
        chosen = slots == places
        picks.append(chosen.astype(BF16))
        if scale_ref is not None:
            scale = jnp.where(chosen, scale_ref[pl.ds(expert, 1), :], 0.0)
            scales.append(jnp.sum(scale, axis=1, keepdims=True))
    rows = dot(jnp.concatenate(picks, axis=0), values_ref[...])
    if scale_ref is not None:
        rows = rows * jnp.concatenate(scales, axis=0)
    for index in range(count):
        for which, out_ref in enumerate(outs):
            start = index * capacity + which * half
            part = rows[start : start + half]
            out_ref[index * half : (index + 1) * half, :] = part.astype(BF16)


def pack(places, scales, values, capacity):
    experts, rows = places.shape
    width = values.shape[1]
    half = capacity // HALVES
    whole = lambda shape: pl.BlockSpec(shape, lambda e: (0, 0))
    operands = [places, values] if scales is None else [places, scales, values]
    count = min(PACK_EXPERTS, experts)
    kernel = functools.partial(pack_kernel, count)
    if scales is None:
        kernel = lambda place_ref, values_ref, *outs: pack_kernel(
            count, place_ref, None, values_ref, *outs
        )
    return pl.pallas_call(
        kernel,
        grid=(experts // count,),
        in_specs=[whole(o.shape) for o in operands],
        out_specs=[pl.BlockSpec((count * half, width), lambda e: (e, 0))] * HALVES,
        out_shape=[jax.ShapeDtypeStruct((experts * half, width), BF16)] * HALVES,
        compiler_params=pltpu.CompilerParams(vmem_limit_bytes=VMEM_BYTES),
        cost_estimate=pl.CostEstimate(
            flops=2 * experts * capacity * rows * width,
            transcendentals=0,
            bytes_accessed=2 * width * (rows + experts * capacity),
        ),
        name="pack",
    )(*operands)


def combine_kernel(experts, capacity, place_ref, scale_ref, first_ref, second_ref, out_ref):
    half = capacity // HALVES
    total = None
    tokens = out_ref.shape[0]
    slots = lax.broadcasted_iota(jnp.int32, (tokens, capacity), 1)
    for expert in range(experts):
        scale = 1.0 if scale_ref is None else scale_ref[:, expert : expert + 1]
        chosen = jnp.where(slots == place_ref[:, expert : expert + 1], scale, 0.0)
        span = slice(expert * half, (expert + 1) * half)
        rows = jnp.concatenate([first_ref[span, :], second_ref[span, :]], axis=0)
        part = dot(chosen.astype(BF16), rows)
        total = part if total is None else total + part
    out_ref[...] = total


def combine(places, scales, rows, capacity):
    tokens, experts = places.shape
    width = rows[0].shape[1]
    block = min(COMBINE_ROWS, tokens)
    part = pl.BlockSpec((block, experts), lambda i: (i, 0))
    kernel = functools.partial(combine_kernel, experts, capacity)
    operands = [places] if scales is None else [places, scales]
    if scales is None:
        kernel = lambda place_ref, *refs: combine_kernel(
            experts, capacity, place_ref, None, *refs
        )
    return pl.pallas_call(
        kernel,
        grid=(tokens // block,),
        in_specs=[part] * len(operands)
        + [pl.BlockSpec(r.shape, lambda i: (0, 0), pipeline_mode=pl.Buffered(1)) for r in rows],
        out_specs=pl.BlockSpec((block, width), lambda i: (i, 0)),
        out_shape=jax.ShapeDtypeStruct((tokens, width), F32),
        compiler_params=pltpu.CompilerParams(vmem_limit_bytes=VMEM_BYTES),
        cost_estimate=pl.CostEstimate(
            flops=2 * experts * capacity * tokens * width,
            transcendentals=0,
            bytes_accessed=2 * width * (2 * tokens + experts * capacity),
        ),
        name="combine",
    )(*operands, *rows)


def gelu_both(hidden):
    inner = 0.7978845608028654
    square = hidden * hidden
    bend = jnp.tanh(hidden * (inner + (inner * 0.044715) * square))
    half = 0.5 + 0.5 * bend
    slope = half + (0.5 * hidden) * (1.0 - bend * bend) * (inner + (3 * inner * 0.044715) * square)
    return hidden * half, slope


def feed_kernel(
    transposed, tile, with_out, in_ref, grad_ref, up_ref, down_ref, act_ref, hid_ref, back_ref, *out
):
    rows, grads = in_ref[...], grad_ref[...]
    hidden_size = act_ref.shape[1]
    for start in range(0, hidden_size, tile):
        part = slice(start, start + tile)
        if transposed:
            hidden = dot(rows, up_ref[part, :], NT)
            grad = dot(grads, down_ref[start // tile])
        else:
            hidden = dot(rows, up_ref[:, part])
            grad = dot(grads, down_ref[part, :], NT)
        active, slope = gelu_both(hidden)
        act_ref[:, part] = active.astype(BF16)
        hid_ref[:, part] = (grad * slope).astype(BF16)
    back = dot(hid_ref[...], up_ref[...], NN if transposed else NT)
    back_ref[...] = back.astype(back_ref.dtype)
    if with_out and not transposed:
        out[0][...] = dot(act_ref[...], down_ref[...]).astype(out[0].dtype)
    if with_out and transposed:
        made = [
            dot(act_ref[:, p * tile : (p + 1) * tile], down_ref[p], NT)
            for p in range(hidden_size // tile)
        ]
        out[0][...] = sum(made).astype(out[0].dtype)


def feed(rows, grads, up, down, transposed, out_dtype, with_out):
    count, width = rows.shape
    hidden_size = up.shape[0] if transposed else up.shape[1]
    block = min(FEED_ROWS, count)
    row = pl.BlockSpec((block, width), lambda i: (i, 0))
    hid = pl.BlockSpec((block, hidden_size), lambda i: (i, 0))
    fixed = lambda a: pl.BlockSpec(a.shape, lambda i: (0,) * a.ndim, pipeline_mode=pl.Buffered(1))
    tile = width if transposed else min(FEED_TILE, hidden_size)
    extra = 1 if with_out else 0
    return pl.pallas_call(
        functools.partial(feed_kernel, transposed, tile, with_out),
        grid=(count // block,),
        in_specs=[row, row, fixed(up), fixed(down)],
        out_specs=[hid, hid, row] + [row] * extra,
        out_shape=[
            jax.ShapeDtypeStruct((count, hidden_size), BF16),
            jax.ShapeDtypeStruct((count, hidden_size), BF16),
            jax.ShapeDtypeStruct((count, width), out_dtype),
        ]
        + [jax.ShapeDtypeStruct((count, width), out_dtype)] * extra,
        compiler_params=pltpu.CompilerParams(vmem_limit_bytes=VMEM_BYTES),
        cost_estimate=pl.CostEstimate(
            flops=(6 + 2 * extra) * count * width * hidden_size,
            transcendentals=count * hidden_size,
            bytes_accessed=4 * count * hidden_size + 8 * count * width + 4 * width * hidden_size,
        ),
        name="feed",
    )(rows, grads, up, down)


def swap(values):
    return lax.ppermute(values, "narrow", [(0, 1), (1, 0)])


def other_narrow(values):
    if lax.axis_size("narrow") != 2:
        return lax.all_gather(values, "narrow", axis=0, tiled=False)
    return swap(values)


def merge_narrow(values, other, axis):
    if lax.axis_size("narrow") != 2:
        return jnp.concatenate([other[i] for i in range(other.shape[0])], axis=axis)
    return jnp.where(
        lax.axis_index("narrow") == 0,
        jnp.concatenate([values, other], axis=axis),
        jnp.concatenate([other, values], axis=axis),
    )


def in_narrow_order(values, other):
    if lax.axis_size("narrow") != 2:
        return [other[i] for i in range(other.shape[0])]
    first = lax.axis_index("narrow") == 0
    return [jnp.where(first, values, other), jnp.where(first, other, values)]


def gather_narrow(values, axis):
    return merge_narrow(values, other_narrow(values), axis)


def part_of(values, index, size, axis):
    return lax.dynamic_slice_in_dim(values, index * size, size, axis)


def reduce_narrow(values, axis):
    count = lax.axis_size("narrow")
    if count != 2:
        return lax.psum_scatter(
            values.astype(BF16), "narrow", scatter_dimension=axis, tiled=True
        ).astype(F32)
    size = values.shape[axis] // 2
    index = lax.axis_index("narrow")
    other = swap(part_of(values, 1 - index, size, axis).astype(BF16))
    return part_of(values, index, size, axis).astype(F32) + other.astype(F32)


def together(*values):
    return lax.optimization_barrier(values)


def to_all(blocks):
    return lax.all_to_all(blocks, "wide", split_axis=0, concat_axis=0, tiled=True)


def exchange(rows):
    wide = lax.axis_size("wide")
    blocks = rows.reshape(wide, rows.shape[0] // wide, rows.shape[1])
    return to_all(blocks).reshape(rows.shape)


def add_narrow(values, other):
    if lax.axis_size("narrow") != 2:
        return reduce_narrow(values, 0)
    own = part_of(values, lax.axis_index("narrow"), other.shape[0], 0)
    return own.astype(F32) + other.astype(F32)


def join_halves(first, second, experts):
    width = first.shape[1]
    parts = [h.reshape(experts, -1, width) for h in (first, second)]
    return jnp.concatenate(parts, axis=1).reshape(-1, width)


def split_halves(rows, experts):
    width = rows.shape[1]
    parts = jnp.split(rows.reshape(experts, -1, width), 2, axis=1)
    return [p.reshape(-1, width) for p in parts]


def gather_wide(values):
    return lax.all_gather(values, "wide", axis=0, tiled=True)


def reduce_wide(values):
    return lax.psum_scatter(values, "wide", scatter_dimension=0, tiled=True)


def on_device(
    patches,
    conditions,
    modulation_weight,
    attention_weight,
    projection_weight,
    expand_weight,
    contract_weight,
    expert_expand,
    expert_contract,
    image_start,
    routes,
    route_gates,
    cotangent,
):
    local_rows, width = patches.shape
    slots = conditions.shape[0]
    experts = lax.axis_size("wide")
    narrow = lax.axis_size("narrow")
    capacity = 4 * local_rows // experts
    mine = lax.axis_index("narrow")
    group_slots = narrow * slots
    group_rows = narrow * local_rows

    modulation_columns = gather_narrow(modulation_weight, 0)
    spread = jnp.broadcast_to(conditions[None], (experts, slots, width))
    all_conditions = gather_narrow(to_all(spread)[:, None], 1).reshape(-1, width)
    half = width // narrow
    attention_end, column_share = attention_weight.shape[1], projection_weight.shape[1]
    expand_share = expand_weight.shape[1]
    folds = contract_weight.shape[0] // half
    hidden_size = narrow * contract_weight.shape[0]
    pieces = hidden_size // width
    early_shard = gather_narrow(
        jnp.concatenate([attention_weight.T, projection_weight.T], axis=0), 1
    )
    contract_shard = contract_weight.T.reshape(column_share, folds, half).transpose(1, 0, 2)
    late_shard = jnp.concatenate([expand_weight.T, contract_shard.reshape(-1, half)], axis=1)
    late_shards = other_narrow(late_shard)
    late_shards = in_narrow_order(late_shard, late_shards)
    late_both, early_shard = together(jnp.concatenate(late_shards, axis=1), early_shard)
    early = gather_wide(early_shard).reshape(experts, -1, width)
    late_both = gather_wide(late_both)
    attention_t = early[:, :attention_end].reshape(3 * width, width)
    projection_t = early[:, attention_end:].reshape(width, width)
    ready_patches, all_conditions, modulation_columns = together(
        patches, all_conditions, modulation_columns
    )
    group_patches = gather_narrow(ready_patches, 0)
    ready_up, ready_down, group_patches = together(
        expert_expand[0], expert_contract[0], group_patches
    )
    other_up, other_down = other_narrow(ready_up), other_narrow(ready_down)

    lifted = jax.nn.silu(all_conditions.astype(F32)).astype(BF16)
    columns = jnp.dot(lifted, modulation_columns, preferred_element_type=F32)
    share = columns.shape[1]
    modulation = to_all(columns.reshape(experts, group_slots, share))
    modulation = modulation.transpose(1, 0, 2).reshape(group_slots, 6, 1, width)
    own = part_of(modulation, mine, slots, 0)
    shift_a, scale_a, gate_a, shift_b, scale_b, gate_b = [own[:, i] for i in range(6)]

    expert_ids = jnp.arange(experts, dtype=jnp.int32)[None, :]
    named = routes[:, :, None] == expert_ids[None]
    chosen = jnp.any(named, axis=1)
    order = jnp.arange(local_rows, dtype=jnp.int32)
    earlier = (order[:, None] > order[None, :]).astype(BF16)
    rank = jnp.dot(earlier, chosen.astype(BF16), preferred_element_type=F32).astype(jnp.int32)
    places = jnp.where(chosen, rank, -1)
    gates = jnp.sum(jnp.where(named, route_gates[:, :, None], 0.0), axis=1)
    places_t, gates_t = places.T, gates.T

    grad_top = cotangent.astype(F32).reshape(slots, IMG_SHORT, width)
    grad_shared = (gate_b * grad_top).astype(BF16).reshape(local_rows, width)
    grad_packed = pack(places_t, gates_t, grad_shared, capacity)
    grad_first, attention_t = together(grad_packed[0], attention_t)
    grad_arrived = [exchange(grad_first)]

    block_start = image_start.reshape(group_slots, IMG_SHORT)[:, 0]
    own_start = part_of(block_start, mine, slots, 0)
    low = own_start - block_start[0]
    high = low + jnp.sum(own_start[:, None] == block_start[None, :], axis=1, dtype=jnp.int32)
    group_inputs = group_patches.astype(F32).reshape(group_slots, IMG_SHORT, width)
    group_entry = (
        (normalize(group_inputs) * (1.0 + modulation[:, 1]) + modulation[:, 0])
        .astype(BF16)
        .reshape(group_rows, width)
    )
    first_entry = part_of(group_entry, mine, local_rows, 0)
    query_t, key_value_t = attention_t[:width], attention_t[width:]
    queries = product(first_entry, query_t, "td,ed->te").astype(BF16)
    keys = product(group_entry, attention_t[width : 2 * width], "td,ed->te").astype(BF16)
    values = product(group_entry, attention_t[2 * width :], "td,ed->te").astype(BF16)
    mixed_heads, exact_heads, totals = attention_forward(queries, keys, values, low, high)
    grad_last, mixed_heads, grad_arrived[0], other_down = together(
        grad_packed[1], mixed_heads, grad_arrived[0], other_down
    )
    grad_arrived.append(exchange(grad_last))
    attended = product(mixed_heads, projection_t, "td,ed->te").reshape(slots, IMG_SHORT, width)
    inputs = patches.astype(F32).reshape(slots, IMG_SHORT, width)
    middle = inputs + gate_a * attended
    normed_b = normalize(middle)
    second = (normed_b * (1.0 + scale_b) + shift_b).astype(BF16).reshape(local_rows, width)

    packed = list(pack(places_t, None, second, capacity))
    packed[0], grad_arrived[1], other_up = together(packed[0], grad_arrived[1], other_up)
    arrived = [exchange(packed[0])]
    halves = jnp.split(late_both, narrow, axis=1)
    expand_t = jnp.concatenate([h[:, :half] for h in halves], axis=1)
    columns = [h[:, half:].reshape(experts, folds, column_share, half) for h in halves]
    columns = [c[:, k].reshape(width, half) for c in columns for k in range(folds)]
    contract_t = jnp.stack(
        [jnp.concatenate(columns[p * narrow : (p + 1) * narrow], axis=1) for p in range(pieces)]
    )
    activated, grad_hidden, grad_second, shared = feed(
        second, grad_shared, expand_t, contract_t, True, F32, True
    )
    up = merge_narrow(expert_expand[0], other_up, 0)
    down = merge_narrow(expert_contract[0], other_down, 0)
    last_packed, grad_second, up, down, arrived[0] = together(
        packed[1], grad_second, up, down, arrived[0]
    )
    arrived.append(exchange(last_packed))
    spans = [slice(i * half, (i + 1) * half) for i in range(hidden_size // half)]
    contract_grads = [
        product(grad_shared, activated[:, span], "td,tf->df")
        .astype(BF16)
        .reshape(experts, column_share, half)
        for span in spans
    ]
    expand_grads = [
        product(grad_hidden, second[:, span], "tf,td->fd").astype(BF16).reshape(experts, -1, half)
        for span in spans[:narrow]
    ]
    shared_grads = jnp.stack(
        [
            jnp.concatenate(
                [expand_grads[i], *contract_grads[i * folds : (i + 1) * folds]], axis=1
            )
            for i in range(narrow)
        ]
    )
    shared_grads = shared_grads.reshape(narrow, -1, half)
    other_shared = swap(part_of(shared_grads, 1 - mine, 1, 0)) if narrow == 2 else shared_grads
    fed = feed(arrived[0], grad_arrived[0], up, down, False, BF16, True)
    grad_ready, arrived[1] = together(fed[2], arrived[1])
    grad_returned = [exchange(grad_ready)]
    fed_last = feed(arrived[1], grad_arrived[1], up, down, False, BF16, True)
    grad_ready, grad_returned[0], other_shared = together(
        fed_last[2], grad_returned[0], other_shared
    )
    shared_sum = add_narrow(shared_grads, other_shared)[0].astype(BF16)
    grad_returned.append(exchange(grad_ready))
    expert_active, grad_expert_hidden = (fed[0], fed_last[0]), (fed[1], fed_last[1])
    produced = join_halves(fed[3], fed_last[3], experts)
    down_grad = sum(product(a, g, "rf,rd->fd") for a, g in zip(expert_active, grad_arrived))
    up_grad = sum(product(a, g, "rd,rf->df") for a, g in zip(arrived, grad_expert_hidden))
    send_up = part_of(up_grad, 1 - mine, half, 0) if narrow == 2 else up_grad
    send_down = part_of(down_grad, 1 - mine, hidden_size // 2, 0) if narrow == 2 else down_grad
    *grad_returned, send_up, send_down, produced, shared_sum = together(
        *grad_returned, send_up.astype(BF16), send_down.astype(BF16), produced, shared_sum
    )
    returned = produced
    returned = exchange(returned)

    shared_sum = reduce_wide(shared_sum)
    other_up_grad = swap(send_up) if narrow == 2 else send_up
    other_down_grad = swap(send_down) if narrow == 2 else send_down

    grad_second = grad_second + combine(places, None, grad_returned, capacity)
    grad_second = grad_second.reshape(slots, IMG_SHORT, width)
    grad_shift_b = jnp.sum(grad_second, axis=1)
    grad_scale_b = jnp.sum(grad_second * normed_b, axis=1)
    grad_middle = grad_top + norm_back(middle, grad_second * (1.0 + scale_b))
    grad_gate_a = jnp.sum(grad_middle * attended, axis=1)
    grad_attended = (gate_a * grad_middle).reshape(local_rows, width).astype(BF16)
    projection_grad_t = product(grad_attended, mixed_heads, "te,td->ed").astype(BF16)
    grad_mixed = product(grad_attended, projection_t, "te,ed->td").astype(BF16)
    grad_queries, grad_keys, grad_values = attention_backward(
        queries, keys, values, grad_mixed, exact_heads, totals, low, high
    )

    other_up_grad, other_down_grad, grad_queries, grad_keys, grad_values = together(
        other_up_grad, other_down_grad, grad_queries, grad_keys, grad_values
    )
    expert_up_grad = add_narrow(up_grad, other_up_grad)[None]
    expert_down_grad = add_narrow(down_grad, other_down_grad)[None]
    returned, expert_up_grad, expert_down_grad = together(
        returned, expert_up_grad, expert_down_grad
    )
    returned = split_halves(returned, experts)
    mixture = shared + combine(places, gates, returned, capacity)
    mixture = mixture.reshape(slots, IMG_SHORT, width)
    attention_grad_t = jnp.concatenate(
        [
            product(grad_queries, first_entry, "te,td->ed").astype(BF16),
            product(grad_keys, group_entry, "te,td->ed").astype(BF16),
            product(grad_values, group_entry, "te,td->ed").astype(BF16),
        ],
        axis=0,
    )
    late_grads = jnp.concatenate(
        [
            attention_grad_t.reshape(experts, attention_end, width),
            projection_grad_t.reshape(experts, column_share, width),
        ],
        axis=1,
    )
    late_grads = late_grads.reshape(-1, width)
    late_grads, grad_queries, grad_keys, grad_values = together(
        late_grads, grad_queries, grad_keys, grad_values
    )
    late_sum = reduce_wide(late_grads)
    grad_group = product(grad_keys, attention_t[width : 2 * width], "te,ed->td") + product(
        grad_values, attention_t[2 * width :], "te,ed->td"
    )
    grad_own = product(grad_queries, query_t, "te,ed->td")
    if narrow == 2:
        other_entry = swap(part_of(grad_group, 1 - mine, local_rows, 0).astype(BF16))
        other_entry, mixture = together(other_entry, mixture)
        grad_entry = add_narrow(grad_group, other_entry) + grad_own
    else:
        grad_entry = reduce_narrow(grad_group, 0) + grad_own
    block_out = (middle + gate_b * mixture).reshape(local_rows, width).astype(BF16)
    grad_gate_b = jnp.sum(grad_top * mixture, axis=1)
    grad_entry = grad_entry.reshape(slots, IMG_SHORT, width)
    grad_shift_a = jnp.sum(grad_entry, axis=1)
    grad_scale_a = jnp.sum(grad_entry * normalize(inputs), axis=1)
    grad_inputs = grad_middle + norm_back(inputs, grad_entry * (1.0 + scale_a))
    patch_grad = grad_inputs.reshape(local_rows, width).astype(BF16)

    grad_modulation = jnp.stack(
        [grad_shift_a, grad_scale_a, grad_gate_a, grad_shift_b, grad_scale_b, grad_gate_b], axis=1
    )
    grad_modulation = grad_modulation.reshape(slots, experts, share).astype(BF16)
    grad_modulation = gather_narrow(to_all(grad_modulation.transpose(1, 0, 2))[:, None], 1)
    row_share = width // narrow
    modulation_grad = product(
        part_of(lifted, mine, row_share, 1),
        grad_modulation.reshape(experts * group_slots, share),
        "sd,se->de",
    )
    expand_share = expand_weight.shape[1]
    expand_grad = shared_sum[:expand_share].astype(F32).T
    contract_grad = shared_sum[expand_share:].astype(F32).reshape(folds, column_share, half)
    contract_grad = contract_grad.transpose(0, 2, 1).reshape(folds * half, column_share)
    late_sum, block_out, patch_grad, modulation_grad, expand_grad, contract_grad = together(
        late_sum, block_out, patch_grad, modulation_grad, expand_grad, contract_grad
    )
    late_sum = reduce_narrow(late_sum, 1).T
    attention_grad, projection_grad = late_sum[:, :attention_end], late_sum[:, attention_end:]
    return (
        block_out,
        patch_grad,
        modulation_grad,
        attention_grad,
        projection_grad,
        expand_grad,
        contract_grad,
        expert_up_grad,
        expert_down_grad,
    )


def solution(mesh):
    rows = P(("wide", "narrow"), None)
    dense = P("narrow", "wide")
    expert = P("wide", "narrow", None)
    return jax.shard_map(
        on_device,
        mesh=mesh,
        in_specs=(rows, rows, dense, dense, dense, dense, dense, expert, expert, P("wide"), rows, rows, rows),
        out_specs=(rows, rows, dense, dense, dense, dense, dense, expert, expert),
        check_vma=False,
    )
```

```python
import functools

import jax
import jax.numpy as jnp
from jax import lax
from jax.experimental import pallas as pl
from jax.experimental.pallas import tpu as pltpu
from jax.sharding import PartitionSpec as P

HEADS = 12
IMG_SHORT = 256
EPSILON = 1e-06
QUAD = 4
HALVES = 2
FORWARD_CHUNK = 512
BACKWARD_CHUNK = 2048
FEED_ROWS = 512
FEED_TILE = 768
PACK_EXPERTS = 2
COMBINE_ROWS = 256
F32 = jnp.float32
BF16 = jnp.bfloat16
NN = (((1,), (0,)), ((), ()))
NT = (((1,), (1,)), ((), ()))
VMEM_BYTES = 48 << 20


def dot(left, right, dims=NN):
    return lax.dot_general(left, right, dims, preferred_element_type=F32)


def product(left, right, form):
    return jnp.einsum(form, left, right, preferred_element_type=F32)


def normalize(values):
    centered = values - jnp.mean(values, axis=-1, keepdims=True)
    variance = jnp.mean(centered * centered, axis=-1, keepdims=True)
    return centered * lax.rsqrt(variance + EPSILON)


def norm_back(values, grad_normed):
    centered = values - jnp.mean(values, axis=-1, keepdims=True)
    variance = jnp.mean(centered * centered, axis=-1, keepdims=True)
    inverse = lax.rsqrt(variance + EPSILON)
    normed = centered * inverse
    return inverse * (
        grad_normed
        - jnp.mean(grad_normed, axis=-1, keepdims=True)
        - normed * jnp.mean(grad_normed * normed, axis=-1, keepdims=True)
    )


def of_head(values, which, axis, head_dim):
    place = lax.broadcasted_iota(jnp.int32, values.shape, axis) // head_dim
    return jnp.where(place == which, values, jnp.zeros_like(values))


def over_keys(low, high, key_rows, chunk, step, state):
    def unrolled():
        inner = state
        for start in range(0, key_rows, chunk):
            inner = step(start, chunk, inner)
        return inner

    def looped():
        first, inner = low, state
        for count in (4, 2, 1):
            size = count * IMG_SHORT
            if size > key_rows:
                continue
            turns = (high - first) // count

            def body(index, inner, first=first, count=count, size=size):
                start = (first + index * count) * IMG_SHORT
                return step(pl.multiple_of(start, IMG_SHORT), size, inner)

            inner = lax.fori_loop(0, turns, body, inner)
            first = first + turns * count
        return inner

    return lax.cond((high - low) * IMG_SHORT == key_rows, unrolled, looped)


def forward_kernel(
    head_dim, low_ref, high_ref, q_ref, k_ref, v_ref, out_ref, exact_ref, total_ref, vt, kept
):
    row_block = pl.program_id(1)

    @pl.when(row_block == 0)
    def _():
        vt[...] = v_ref[...].T

    queries = (q_ref[...].astype(F32) * head_dim**-0.5).astype(BF16).T
    rows = q_ref.shape[0]
    by_head = [of_head(queries, h, 0, head_dim) for h in range(QUAD)]
    low, high = low_ref[row_block], high_ref[row_block]
    key_rows = k_ref.shape[0]

    def score_step(at, size, tops):
        keys = k_ref[pl.ds(at, size), :]
        fresh = []
        for h in range(QUAD):
            scores = dot(keys, by_head[h])
            kept[h, pl.ds(at, size), :] = scores
            fresh.append(
                jnp.maximum(tops[h], jnp.max(scores.reshape(size // 8, 8, rows), axis=0))
            )
        return tuple(fresh)

    chunk = min(FORWARD_CHUNK, key_rows)
    tops = over_keys(
        low, high, key_rows, chunk, score_step, tuple(jnp.full((8, rows), -1e30, F32) for _ in range(QUAD))
    )
    tops = [jnp.max(t, axis=0, keepdims=True) for t in tops]

    def mix_step(at, size, state):
        fresh = []
        for h in range(QUAD):
            total, mixed = state[h]
            weights = jnp.exp(kept[h, pl.ds(at, size), :] - tops[h])
            total = total + jnp.sum(weights.reshape(size // 8, 8, rows), axis=0)
            values = vt[h * head_dim : (h + 1) * head_dim, pl.ds(at, size)]
            fresh.append((total, mixed + dot(values, weights.astype(BF16))))
        return tuple(fresh)

    state = over_keys(
        low,
        high,
        key_rows,
        chunk,
        mix_step,
        tuple((jnp.zeros((8, rows), F32), jnp.zeros((head_dim, rows), F32)) for _ in range(QUAD)),
    )
    mixed = []
    for h in range(QUAD):
        total = jnp.sum(state[h][0], axis=0, keepdims=True)
        mixed.append(state[h][1] / total)
        total_ref[0, h : h + 1, :] = tops[h] + jnp.log(total)
    mixed = jnp.concatenate(mixed, axis=0).T
    exact_ref[...] = mixed
    out_ref[...] = mixed.astype(BF16)


def attention_forward(queries, keys, values, low, high):
    rows, width = queries.shape
    key_rows = keys.shape[0]
    head_dim = width // HEADS
    lanes, quads = QUAD * head_dim, HEADS // QUAD
    size = IMG_SHORT
    row_spec = pl.BlockSpec((size, lanes), lambda j, i, *_: (i, j))
    key_spec = pl.BlockSpec((key_rows, lanes), lambda j, i, *_: (0, j))
    return pl.pallas_call(
        functools.partial(forward_kernel, head_dim),
        grid_spec=pltpu.PrefetchScalarGridSpec(
            num_scalar_prefetch=2,
            grid=(quads, rows // size),
            in_specs=[row_spec, key_spec, key_spec],
            out_specs=[
                row_spec,
                row_spec,
                pl.BlockSpec((1, QUAD, size), lambda j, i, *_: (j, 0, i)),
            ],
            scratch_shapes=[
                pltpu.VMEM((lanes, key_rows), BF16),
                pltpu.VMEM((QUAD, key_rows, size), F32),
            ],
        ),
        out_shape=[
            jax.ShapeDtypeStruct((rows, width), BF16),
            jax.ShapeDtypeStruct((rows, width), F32),
            jax.ShapeDtypeStruct((quads, QUAD, rows), F32),
        ],
        compiler_params=pltpu.CompilerParams(vmem_limit_bytes=VMEM_BYTES),
        cost_estimate=pl.CostEstimate(
            flops=16 * rows * key_rows * width,
            transcendentals=rows * key_rows * HEADS,
            bytes_accessed=4 * key_rows * width + 8 * rows * width,
        ),
        name="attention_forward",
    )(low, high, queries, keys, values)


def backward_kernel(
    head_dim,
    low_ref,
    high_ref,
    q_ref,
    k_ref,
    v_ref,
    grad_ref,
    exact_ref,
    total_ref,
    dq_ref,
    dk_ref,
    dv_ref,
    kt,
    dk_sum,
    dv_sum,
):
    row_block = pl.program_id(1)

    @pl.when(row_block == 0)
    def _():
        kt[...] = k_ref[...].T
        dk_sum[...] = jnp.zeros_like(dk_sum)
        dv_sum[...] = jnp.zeros_like(dv_sum)

    scale = head_dim**-0.5
    queries = (q_ref[...].astype(F32) * scale).astype(BF16)
    grads = grad_ref[...]
    rows = queries.shape[0]
    heads = range(QUAD)
    dots = (grads.astype(F32) * exact_ref[...]).T
    dots = [
        jnp.sum(dots[h * head_dim : (h + 1) * head_dim], axis=0, keepdims=True) for h in heads
    ]
    q_columns, g_columns = queries.T, grads.T
    q_columns = [of_head(q_columns, h, 0, head_dim) for h in heads]
    g_columns = [of_head(g_columns, h, 0, head_dim) for h in heads]
    q_rows = jnp.concatenate([of_head(queries, h, 1, head_dim) for h in heads], axis=0)
    g_rows = jnp.concatenate([of_head(grads, h, 1, head_dim) for h in heads], axis=0)
    totals = [total_ref[0, h : h + 1, :] for h in heads]
    low, high = low_ref[row_block], high_ref[row_block]
    key_rows = k_ref.shape[0]

    def step(at, size, dq):
        keys = k_ref[pl.ds(at, size), :]
        values = v_ref[pl.ds(at, size), :]
        weights, score_grads, fresh = [], [], []
        for h in heads:
            softmax = jnp.exp(dot(keys, q_columns[h]) - totals[h])
            grad = (softmax * (dot(values, g_columns[h]) - dots[h])).astype(BF16)
            weights.append(softmax.astype(BF16))
            score_grads.append(grad)
            columns = kt[h * head_dim : (h + 1) * head_dim, pl.ds(at, size)]
            fresh.append(dq[h] + dot(columns, grad))
        dv_sum[pl.ds(at, size), :] += dot(jnp.concatenate(weights, axis=1), g_rows)
        dk_sum[pl.ds(at, size), :] += dot(jnp.concatenate(score_grads, axis=1), q_rows)
        return tuple(fresh)

    chunk = min(BACKWARD_CHUNK, key_rows)
    dq = over_keys(
        low, high, key_rows, chunk, step, tuple(jnp.zeros((head_dim, rows), F32) for _ in heads)
    )
    dq_ref[...] = (jnp.concatenate(dq, axis=0) * scale).T.astype(BF16)

    @pl.when(row_block == pl.num_programs(1) - 1)
    def _():
        dk_ref[...] = dk_sum[...].astype(BF16)
        dv_ref[...] = dv_sum[...].astype(BF16)


def attention_backward(queries, keys, values, grads, exact, totals, low, high):
    rows, width = queries.shape
    key_rows = keys.shape[0]
    head_dim = width // HEADS
    lanes, quads = QUAD * head_dim, HEADS // QUAD
    size = IMG_SHORT
    row_spec = pl.BlockSpec((size, lanes), lambda j, i, *_: (i, j))
    key_spec = pl.BlockSpec((key_rows, lanes), lambda j, i, *_: (0, j))
    return pl.pallas_call(
        functools.partial(backward_kernel, head_dim),
        grid_spec=pltpu.PrefetchScalarGridSpec(
            num_scalar_prefetch=2,
            grid=(quads, rows // size),
            in_specs=[
                row_spec,
                key_spec,
                key_spec,
                row_spec,
                row_spec,
                pl.BlockSpec((1, QUAD, size), lambda j, i, *_: (j, 0, i)),
            ],
            out_specs=[row_spec, key_spec, key_spec],
            scratch_shapes=[
                pltpu.VMEM((lanes, key_rows), BF16),
                pltpu.VMEM((key_rows, lanes), F32),
                pltpu.VMEM((key_rows, lanes), F32),
            ],
        ),
        out_shape=[
            jax.ShapeDtypeStruct((rows, width), BF16),
            jax.ShapeDtypeStruct((key_rows, width), BF16),
            jax.ShapeDtypeStruct((key_rows, width), BF16),
        ],
        compiler_params=pltpu.CompilerParams(vmem_limit_bytes=VMEM_BYTES),
        cost_estimate=pl.CostEstimate(
            flops=40 * rows * key_rows * width,
            transcendentals=rows * key_rows * HEADS,
            bytes_accessed=8 * key_rows * width + 10 * rows * width,
        ),
        name="attention_backward",
    )(low, high, queries, keys, values, grads, exact, totals)


def pack_kernel(count, place_ref, scale_ref, values_ref, *outs):
    half = outs[0].shape[0] // count
    capacity = half * len(outs)
    picks, scales = [], []
    for index in range(count):
        expert = pl.program_id(0) * count + index
        places = place_ref[pl.ds(expert, 1), :]
        slots = lax.broadcasted_iota(jnp.int32, (capacity, places.shape[1]), 0)
        chosen = slots == places
        picks.append(chosen.astype(BF16))
        if scale_ref is not None:
            scale = jnp.where(chosen, scale_ref[pl.ds(expert, 1), :], 0.0)
            scales.append(jnp.sum(scale, axis=1, keepdims=True))
    rows = dot(jnp.concatenate(picks, axis=0), values_ref[...])
    if scale_ref is not None:
        rows = rows * jnp.concatenate(scales, axis=0)
    for index in range(count):
        for which, out_ref in enumerate(outs):
            start = index * capacity + which * half
            part = rows[start : start + half]
            out_ref[index * half : (index + 1) * half, :] = part.astype(BF16)


def pack(places, scales, values, capacity):
    experts, rows = places.shape
    width = values.shape[1]
    half = capacity // HALVES
    whole = lambda shape: pl.BlockSpec(shape, lambda e: (0, 0))
    operands = [places, values] if scales is None else [places, scales, values]
    count = min(PACK_EXPERTS, experts)
    kernel = functools.partial(pack_kernel, count)
    if scales is None:
        kernel = lambda place_ref, values_ref, *outs: pack_kernel(
            count, place_ref, None, values_ref, *outs
        )
    return pl.pallas_call(
        kernel,
        grid=(experts // count,),
        in_specs=[whole(o.shape) for o in operands],
        out_specs=[pl.BlockSpec((count * half, width), lambda e: (e, 0))] * HALVES,
        out_shape=[jax.ShapeDtypeStruct((experts * half, width), BF16)] * HALVES,
        compiler_params=pltpu.CompilerParams(vmem_limit_bytes=VMEM_BYTES),
        cost_estimate=pl.CostEstimate(
            flops=2 * experts * capacity * rows * width,
            transcendentals=0,
            bytes_accessed=2 * width * (rows + experts * capacity),
        ),
        name="pack",
    )(*operands)


def combine_kernel(experts, capacity, place_ref, scale_ref, first_ref, second_ref, out_ref):
    half = capacity // HALVES
    total = None
    tokens = out_ref.shape[0]
    slots = lax.broadcasted_iota(jnp.int32, (tokens, capacity), 1)
    for expert in range(experts):
        scale = 1.0 if scale_ref is None else scale_ref[:, expert : expert + 1]
        chosen = jnp.where(slots == place_ref[:, expert : expert + 1], scale, 0.0)
        span = slice(expert * half, (expert + 1) * half)
        rows = jnp.concatenate([first_ref[span, :], second_ref[span, :]], axis=0)
        part = dot(chosen.astype(BF16), rows)
        total = part if total is None else total + part
    out_ref[...] = total


def combine(places, scales, rows, capacity):
    tokens, experts = places.shape
    width = rows[0].shape[1]
    block = min(COMBINE_ROWS, tokens)
    part = pl.BlockSpec((block, experts), lambda i: (i, 0))
    kernel = functools.partial(combine_kernel, experts, capacity)
    operands = [places] if scales is None else [places, scales]
    if scales is None:
        kernel = lambda place_ref, *refs: combine_kernel(
            experts, capacity, place_ref, None, *refs
        )
    return pl.pallas_call(
        kernel,
        grid=(tokens // block,),
        in_specs=[part] * len(operands)
        + [pl.BlockSpec(r.shape, lambda i: (0, 0), pipeline_mode=pl.Buffered(1)) for r in rows],
        out_specs=pl.BlockSpec((block, width), lambda i: (i, 0)),
        out_shape=jax.ShapeDtypeStruct((tokens, width), F32),
        compiler_params=pltpu.CompilerParams(vmem_limit_bytes=VMEM_BYTES),
        cost_estimate=pl.CostEstimate(
            flops=2 * experts * capacity * tokens * width,
            transcendentals=0,
            bytes_accessed=2 * width * (2 * tokens + experts * capacity),
        ),
        name="combine",
    )(*operands, *rows)


def gelu_both(hidden):
    inner = 0.7978845608028654
    square = hidden * hidden
    bend = jnp.tanh(hidden * (inner + (inner * 0.044715) * square))
    half = 0.5 + 0.5 * bend
    slope = half + (0.5 * hidden) * (1.0 - bend * bend) * (inner + (3 * inner * 0.044715) * square)
    return hidden * half, slope


def feed_kernel(
    transposed, tile, with_out, in_ref, grad_ref, up_ref, down_ref, act_ref, hid_ref, back_ref, *out
):
    rows, grads = in_ref[...], grad_ref[...]
    hidden_size = act_ref.shape[1]
    for start in range(0, hidden_size, tile):
        part = slice(start, start + tile)
        if transposed:
            hidden = dot(rows, up_ref[part, :], NT)
            grad = dot(grads, down_ref[start // tile])
        else:
            hidden = dot(rows, up_ref[:, part])
            grad = dot(grads, down_ref[part, :], NT)
        active, slope = gelu_both(hidden)
        act_ref[:, part] = active.astype(BF16)
        hid_ref[:, part] = (grad * slope).astype(BF16)
    back = dot(hid_ref[...], up_ref[...], NN if transposed else NT)
    back_ref[...] = back.astype(back_ref.dtype)
    if with_out and not transposed:
        out[0][...] = dot(act_ref[...], down_ref[...]).astype(out[0].dtype)
    if with_out and transposed:
        made = [
            dot(act_ref[:, p * tile : (p + 1) * tile], down_ref[p], NT)
            for p in range(hidden_size // tile)
        ]
        out[0][...] = sum(made).astype(out[0].dtype)


def feed(rows, grads, up, down, transposed, out_dtype, with_out):
    count, width = rows.shape
    hidden_size = up.shape[0] if transposed else up.shape[1]
    block = min(FEED_ROWS, count)
    row = pl.BlockSpec((block, width), lambda i: (i, 0))
    hid = pl.BlockSpec((block, hidden_size), lambda i: (i, 0))
    fixed = lambda a: pl.BlockSpec(a.shape, lambda i: (0,) * a.ndim, pipeline_mode=pl.Buffered(1))
    tile = width if transposed else min(FEED_TILE, hidden_size)
    extra = 1 if with_out else 0
    return pl.pallas_call(
        functools.partial(feed_kernel, transposed, tile, with_out),
        grid=(count // block,),
        in_specs=[row, row, fixed(up), fixed(down)],
        out_specs=[hid, hid, row] + [row] * extra,
        out_shape=[
            jax.ShapeDtypeStruct((count, hidden_size), BF16),
            jax.ShapeDtypeStruct((count, hidden_size), BF16),
            jax.ShapeDtypeStruct((count, width), out_dtype),
        ]
        + [jax.ShapeDtypeStruct((count, width), out_dtype)] * extra,
        compiler_params=pltpu.CompilerParams(vmem_limit_bytes=VMEM_BYTES),
        cost_estimate=pl.CostEstimate(
            flops=(6 + 2 * extra) * count * width * hidden_size,
            transcendentals=count * hidden_size,
            bytes_accessed=4 * count * hidden_size + 8 * count * width + 4 * width * hidden_size,
        ),
        name="feed",
    )(rows, grads, up, down)


def swap(values):
    return lax.ppermute(values, "narrow", [(0, 1), (1, 0)])


def other_narrow(values):
    if lax.axis_size("narrow") != 2:
        return lax.all_gather(values, "narrow", axis=0, tiled=False)
    return swap(values)


def merge_narrow(values, other, axis):
    if lax.axis_size("narrow") != 2:
        return jnp.concatenate([other[i] for i in range(other.shape[0])], axis=axis)
    return jnp.where(
        lax.axis_index("narrow") == 0,
        jnp.concatenate([values, other], axis=axis),
        jnp.concatenate([other, values], axis=axis),
    )


def in_narrow_order(values, other):
    if lax.axis_size("narrow") != 2:
        return [other[i] for i in range(other.shape[0])]
    first = lax.axis_index("narrow") == 0
    return [jnp.where(first, values, other), jnp.where(first, other, values)]


def gather_narrow(values, axis):
    return merge_narrow(values, other_narrow(values), axis)


def part_of(values, index, size, axis):
    return lax.dynamic_slice_in_dim(values, index * size, size, axis)


def reduce_narrow(values, axis):
    count = lax.axis_size("narrow")
    if count != 2:
        return lax.psum_scatter(
            values.astype(BF16), "narrow", scatter_dimension=axis, tiled=True
        ).astype(F32)
    size = values.shape[axis] // 2
    index = lax.axis_index("narrow")
    other = swap(part_of(values, 1 - index, size, axis).astype(BF16))
    return part_of(values, index, size, axis).astype(F32) + other.astype(F32)


def together(*values):
    return lax.optimization_barrier(values)


def to_all(blocks):
    return lax.all_to_all(blocks, "wide", split_axis=0, concat_axis=0, tiled=True)


def exchange(rows):
    wide = lax.axis_size("wide")
    blocks = rows.reshape(wide, rows.shape[0] // wide, rows.shape[1])
    return to_all(blocks).reshape(rows.shape)


def add_narrow(values, other):
    if lax.axis_size("narrow") != 2:
        return reduce_narrow(values, 0)
    own = part_of(values, lax.axis_index("narrow"), other.shape[0], 0)
    return own.astype(F32) + other.astype(F32)


def join_halves(first, second, experts):
    width = first.shape[1]
    parts = [h.reshape(experts, -1, width) for h in (first, second)]
    return jnp.concatenate(parts, axis=1).reshape(-1, width)


def split_halves(rows, experts):
    width = rows.shape[1]
    parts = jnp.split(rows.reshape(experts, -1, width), 2, axis=1)
    return [p.reshape(-1, width) for p in parts]


def gather_wide(values):
    return lax.all_gather(values, "wide", axis=0, tiled=True)


def reduce_wide(values):
    return lax.psum_scatter(values, "wide", scatter_dimension=0, tiled=True)


def on_device(
    patches,
    conditions,
    modulation_weight,
    attention_weight,
    projection_weight,
    expand_weight,
    contract_weight,
    expert_expand,
    expert_contract,
    image_start,
    routes,
    route_gates,
    cotangent,
):
    local_rows, width = patches.shape
    slots = conditions.shape[0]
    experts = lax.axis_size("wide")
    narrow = lax.axis_size("narrow")
    capacity = 4 * local_rows // experts
    mine = lax.axis_index("narrow")
    group_slots = narrow * slots
    group_rows = narrow * local_rows

    modulation_columns = gather_narrow(modulation_weight, 0)
    spread = jnp.broadcast_to(conditions[None], (experts, slots, width))
    all_conditions = gather_narrow(to_all(spread)[:, None], 1).reshape(-1, width)
    half = width // narrow
    attention_end, column_share = attention_weight.shape[1], projection_weight.shape[1]
    expand_share = expand_weight.shape[1]
    folds = contract_weight.shape[0] // half
    hidden_size = narrow * contract_weight.shape[0]
    pieces = hidden_size // width
    early_shard = gather_narrow(
        jnp.concatenate([attention_weight.T, projection_weight.T], axis=0), 1
    )
    contract_shard = contract_weight.T.reshape(column_share, folds, half).transpose(1, 0, 2)
    late_shard = jnp.concatenate([expand_weight.T, contract_shard.reshape(-1, half)], axis=1)
    late_shards = other_narrow(late_shard)
    late_shards = in_narrow_order(late_shard, late_shards)
    late_both, early_shard = together(jnp.concatenate(late_shards, axis=1), early_shard)
    early = gather_wide(early_shard).reshape(experts, -1, width)
    late_both = gather_wide(late_both)
    attention_t = early[:, :attention_end].reshape(3 * width, width)
    projection_t = early[:, attention_end:].reshape(width, width)
    ready_patches, all_conditions, modulation_columns = together(
        patches, all_conditions, modulation_columns
    )
    group_patches = gather_narrow(ready_patches, 0)
    ready_up, ready_down, group_patches = together(
        expert_expand[0], expert_contract[0], group_patches
    )
    other_up, other_down = other_narrow(ready_up), other_narrow(ready_down)

    lifted = jax.nn.silu(all_conditions.astype(F32)).astype(BF16)
    columns = jnp.dot(lifted, modulation_columns, preferred_element_type=F32)
    share = columns.shape[1]
    modulation = to_all(columns.reshape(experts, group_slots, share))
    modulation = modulation.transpose(1, 0, 2).reshape(group_slots, 6, 1, width)
    own = part_of(modulation, mine, slots, 0)
    shift_a, scale_a, gate_a, shift_b, scale_b, gate_b = [own[:, i] for i in range(6)]

    expert_ids = jnp.arange(experts, dtype=jnp.int32)[None, :]
    named = routes[:, :, None] == expert_ids[None]
    chosen = jnp.any(named, axis=1)
    order = jnp.arange(local_rows, dtype=jnp.int32)
    earlier = (order[:, None] > order[None, :]).astype(BF16)
    rank = jnp.dot(earlier, chosen.astype(BF16), preferred_element_type=F32).astype(jnp.int32)
    places = jnp.where(chosen, rank, -1)
    gates = jnp.sum(jnp.where(named, route_gates[:, :, None], 0.0), axis=1)
    places_t, gates_t = places.T, gates.T

    grad_top = cotangent.astype(F32).reshape(slots, IMG_SHORT, width)
    grad_shared = (gate_b * grad_top).astype(BF16).reshape(local_rows, width)
    grad_packed = pack(places_t, gates_t, grad_shared, capacity)
    grad_first, attention_t = together(grad_packed[0], attention_t)
    grad_arrived = [exchange(grad_first)]

    block_start = image_start.reshape(group_slots, IMG_SHORT)[:, 0]
    own_start = part_of(block_start, mine, slots, 0)
    low = own_start - block_start[0]
    high = low + jnp.sum(own_start[:, None] == block_start[None, :], axis=1, dtype=jnp.int32)
    group_inputs = group_patches.astype(F32).reshape(group_slots, IMG_SHORT, width)
    group_entry = (
        (normalize(group_inputs) * (1.0 + modulation[:, 1]) + modulation[:, 0])
        .astype(BF16)
        .reshape(group_rows, width)
    )
    first_entry = part_of(group_entry, mine, local_rows, 0)
    query_t, key_value_t = attention_t[:width], attention_t[width:]
    queries = product(first_entry, query_t, "td,ed->te").astype(BF16)
    keys = product(group_entry, attention_t[width : 2 * width], "td,ed->te").astype(BF16)
    values = product(group_entry, attention_t[2 * width :], "td,ed->te").astype(BF16)
    mixed_heads, exact_heads, totals = attention_forward(queries, keys, values, low, high)
    grad_last, mixed_heads, grad_arrived[0], other_down = together(
        grad_packed[1], mixed_heads, grad_arrived[0], other_down
    )
    grad_arrived.append(exchange(grad_last))
    attended = product(mixed_heads, projection_t, "td,ed->te").reshape(slots, IMG_SHORT, width)
    inputs = patches.astype(F32).reshape(slots, IMG_SHORT, width)
    middle = inputs + gate_a * attended
    normed_b = normalize(middle)
    second = (normed_b * (1.0 + scale_b) + shift_b).astype(BF16).reshape(local_rows, width)

    packed = list(pack(places_t, None, second, capacity))
    packed[0], grad_arrived[1], other_up = together(packed[0], grad_arrived[1], other_up)
    arrived = [exchange(packed[0])]
    halves = jnp.split(late_both, narrow, axis=1)
    expand_t = jnp.concatenate([h[:, :half] for h in halves], axis=1)
    columns = [h[:, half:].reshape(experts, folds, column_share, half) for h in halves]
    columns = [c[:, k].reshape(width, half) for c in columns for k in range(folds)]
    contract_t = jnp.stack(
        [jnp.concatenate(columns[p * narrow : (p + 1) * narrow], axis=1) for p in range(pieces)]
    )
    activated, grad_hidden, grad_second, shared = feed(
        second, grad_shared, expand_t, contract_t, True, F32, True
    )
    up = merge_narrow(expert_expand[0], other_up, 0)
    down = merge_narrow(expert_contract[0], other_down, 0)
    last_packed, grad_second, up, down, arrived[0] = together(
        packed[1], grad_second, up, down, arrived[0]
    )
    arrived.append(exchange(last_packed))
    spans = [slice(i * half, (i + 1) * half) for i in range(hidden_size // half)]
    contract_grads = [
        product(grad_shared, activated[:, span], "td,tf->df")
        .astype(BF16)
        .reshape(experts, column_share, half)
        for span in spans
    ]
    expand_grads = [
        product(grad_hidden, second[:, span], "tf,td->fd").astype(BF16).reshape(experts, -1, half)
        for span in spans[:narrow]
    ]
    shared_grads = jnp.stack(
        [
            jnp.concatenate(
                [expand_grads[i], *contract_grads[i * folds : (i + 1) * folds]], axis=1
            )
            for i in range(narrow)
        ]
    )
    shared_grads = shared_grads.reshape(narrow, -1, half)
    other_shared = swap(part_of(shared_grads, 1 - mine, 1, 0)) if narrow == 2 else shared_grads
    fed = feed(arrived[0], grad_arrived[0], up, down, False, BF16, True)
    grad_ready, arrived[1] = together(fed[2], arrived[1])
    grad_returned = [exchange(grad_ready)]
    fed_last = feed(arrived[1], grad_arrived[1], up, down, False, BF16, True)
    grad_ready, grad_returned[0], other_shared = together(
        fed_last[2], grad_returned[0], other_shared
    )
    shared_sum = add_narrow(shared_grads, other_shared)[0].astype(BF16)
    grad_returned.append(exchange(grad_ready))
    expert_active, grad_expert_hidden = (fed[0], fed_last[0]), (fed[1], fed_last[1])
    produced = join_halves(fed[3], fed_last[3], experts)
    down_grad = sum(product(a, g, "rf,rd->fd") for a, g in zip(expert_active, grad_arrived))
    up_grad = sum(product(a, g, "rd,rf->df") for a, g in zip(arrived, grad_expert_hidden))
    send_up = part_of(up_grad, 1 - mine, half, 0) if narrow == 2 else up_grad
    send_down = part_of(down_grad, 1 - mine, hidden_size // 2, 0) if narrow == 2 else down_grad
    *grad_returned, send_up, send_down, produced, shared_sum = together(
        *grad_returned, send_up.astype(BF16), send_down.astype(BF16), produced, shared_sum
    )
    returned = produced
    returned = exchange(returned)

    shared_sum = reduce_wide(shared_sum)
    other_up_grad = swap(send_up) if narrow == 2 else send_up
    other_down_grad = swap(send_down) if narrow == 2 else send_down

    grad_second = grad_second + combine(places, None, grad_returned, capacity)
    grad_second = grad_second.reshape(slots, IMG_SHORT, width)
    grad_shift_b = jnp.sum(grad_second, axis=1)
    grad_scale_b = jnp.sum(grad_second * normed_b, axis=1)
    grad_middle = grad_top + norm_back(middle, grad_second * (1.0 + scale_b))
    grad_gate_a = jnp.sum(grad_middle * attended, axis=1)
    grad_attended = (gate_a * grad_middle).reshape(local_rows, width).astype(BF16)
    projection_grad_t = product(grad_attended, mixed_heads, "te,td->ed").astype(BF16)
    grad_mixed = product(grad_attended, projection_t, "te,ed->td").astype(BF16)
    grad_queries, grad_keys, grad_values = attention_backward(
        queries, keys, values, grad_mixed, exact_heads, totals, low, high
    )

    other_up_grad, other_down_grad, grad_queries, grad_keys, grad_values = together(
        other_up_grad, other_down_grad, grad_queries, grad_keys, grad_values
    )
    expert_up_grad = add_narrow(up_grad, other_up_grad)[None]
    expert_down_grad = add_narrow(down_grad, other_down_grad)[None]
    returned, expert_up_grad, expert_down_grad = together(
        returned, expert_up_grad, expert_down_grad
    )
    returned = split_halves(returned, experts)
    mixture = shared + combine(places, gates, returned, capacity)
    mixture = mixture.reshape(slots, IMG_SHORT, width)
    attention_grad_t = jnp.concatenate(
        [
            product(grad_queries, first_entry, "te,td->ed").astype(BF16),
            product(grad_keys, group_entry, "te,td->ed").astype(BF16),
            product(grad_values, group_entry, "te,td->ed").astype(BF16),
        ],
        axis=0,
    )
    late_grads = jnp.concatenate(
        [
            attention_grad_t.reshape(experts, attention_end, width),
            projection_grad_t.reshape(experts, column_share, width),
        ],
        axis=1,
    )
    late_grads = late_grads.reshape(-1, width)
    late_grads, grad_queries, grad_keys, grad_values = together(
        late_grads, grad_queries, grad_keys, grad_values
    )
    late_sum = reduce_wide(late_grads)
    grad_group = product(grad_keys, attention_t[width : 2 * width], "te,ed->td") + product(
        grad_values, attention_t[2 * width :], "te,ed->td"
    )
    grad_own = product(grad_queries, query_t, "te,ed->td")
    if narrow == 2:
        other_entry = swap(part_of(grad_group, 1 - mine, local_rows, 0).astype(BF16))
        other_entry, mixture = together(other_entry, mixture)
        grad_entry = add_narrow(grad_group, other_entry) + grad_own
    else:
        grad_entry = reduce_narrow(grad_group, 0) + grad_own
    block_out = (middle + gate_b * mixture).reshape(local_rows, width).astype(BF16)
    grad_gate_b = jnp.sum(grad_top * mixture, axis=1)
    grad_entry = grad_entry.reshape(slots, IMG_SHORT, width)
    grad_shift_a = jnp.sum(grad_entry, axis=1)
    grad_scale_a = jnp.sum(grad_entry * normalize(inputs), axis=1)
    grad_inputs = grad_middle + norm_back(inputs, grad_entry * (1.0 + scale_a))
    patch_grad = grad_inputs.reshape(local_rows, width).astype(BF16)

    grad_modulation = jnp.stack(
        [grad_shift_a, grad_scale_a, grad_gate_a, grad_shift_b, grad_scale_b, grad_gate_b], axis=1
    )
    grad_modulation = grad_modulation.reshape(slots, experts, share).astype(BF16)
    grad_modulation = gather_narrow(to_all(grad_modulation.transpose(1, 0, 2))[:, None], 1)
    row_share = width // narrow
    modulation_grad = product(
        part_of(lifted, mine, row_share, 1),
        grad_modulation.reshape(experts * group_slots, share),
        "sd,se->de",
    )
    expand_share = expand_weight.shape[1]
    expand_grad = shared_sum[:expand_share].astype(F32).T
    contract_grad = shared_sum[expand_share:].astype(F32).reshape(folds, column_share, half)
    contract_grad = contract_grad.transpose(0, 2, 1).reshape(folds * half, column_share)
    late_sum, block_out, patch_grad, modulation_grad, expand_grad, contract_grad = together(
        late_sum, block_out, patch_grad, modulation_grad, expand_grad, contract_grad
    )
    late_sum = reduce_narrow(late_sum, 1).T
    attention_grad, projection_grad = late_sum[:, :attention_end], late_sum[:, attention_end:]
    return (
        block_out,
        patch_grad,
        modulation_grad,
        attention_grad,
        projection_grad,
        expand_grad,
        contract_grad,
        expert_up_grad,
        expert_down_grad,
    )


def solution(mesh):
    rows = P(("wide", "narrow"), None)
    dense = P("narrow", "wide")
    expert = P("wide", "narrow", None)
    return jax.shard_map(
        on_device,
        mesh=mesh,
        in_specs=(rows, rows, dense, dense, dense, dense, dense, expert, expert, P("wide"), rows, rows, rows),
        out_specs=(rows, rows, dense, dense, dense, dense, dense, expert, expert),
        check_vma=False,
    )
```
